32 devices in a mesh: slab: 8 (over z, core), dom: 4 (over y, x).
Axes of the slice: x: 2, y: 2, z: 4, core: 2. Of those that a mesh axis runs over, the one named last changes fastest.
Arguments:
- positions: float32 [3, 16384], P(None, ('slab', 'dom')), may hold values from -0.5 to 32.5, as said below
- burgers: float32 [3, 16384], P(None, ('slab', 'dom')), may hold values from -6 to 6
- mobility: float32 [16384], P(('slab', 'dom')), may hold values from 0.5 to 2
- block_cells: int32 [128], P(('slab', 'dom')), may hold values from 0 to 127, as said below
- pairs: int32 [2048, 2], P(('slab', 'dom')), may hold values from 0 to 127, as said below
- pair_count: int32 [32], P(('slab', 'dom')), may hold values from 8 to 64, as said below
Outputs:
- moved: float32 [3, 16384], P(None, ('slab', 'dom'))
- velocity: float32 [3, 16384], P(None, ('slab', 'dom'))
The draws below stay inside these ranges and needn't reach their ends.
Inputs may be any that keep to these rules, and one draw needn't show every extreme that they name: `block_cells`: block k lies in slab k // (4 * 4) and its cell is 16 times that slab plus 0 to 15. `positions`: each segment lies within 2.5 of its block's cell centre along x and within 1.5 along y and z. `pairs`: device d = s * 4 + e owns blocks d * 4 to (d + 1) * 4 - 1. In device d's slots the first block is one of its own; the second is owned by a device of slab s - 1, s or s + 1 at dom position e - 1, e or e + 1, and differs from the first. Every slot holds such a pair, used or not. `pair_count`: in each slab exactly one device has 64 used slots; the others have at most 32.
All inputs are finite; a program needn't handle non-finite values.
Results may differ from the reference program's by a relative error of at most 0.0003.
Values sent between devices are 32-bit elements; how exact they have to be, the bound alone decides.
No kernel may reach another device: no remote copies, remote signals or barrier semaphores. Data moves between devices by JAX's collectives and lax.ppermute only.
A program may use at most 64 MiB of HBM per device.

```python
import math
import jax
import jax.numpy as jnp
from jax import lax

BLOCK_SEGS = 128
BLK_DEV = 4
MOST_BLOCK_PAIRS = 64
BLOCKS = 128
SEGS = 16384
CELLS = 128
N_SLAB = 8
N_DOM = 4


def cell_helper(key):
    count = BLK_DEV * N_SLAB * N_DOM
    sub = jax.random.fold_in(key, 11)
    slabs = jnp.arange(count, dtype=jnp.int32) // (BLK_DEV * N_DOM)
    return (slabs * 16 + jax.random.randint(sub, (count,), 0, 16)).astype(jnp.int32)


def draw_block_cells(key, part):
    return cell_helper(key)


def draw_positions(key, part):
    cells = cell_helper(key)
    count = cells.shape[0]
    slabs = cells // 16
    rest = cells % 16
    centre = jnp.stack([4 * slabs + 2, 2 * (rest // 4) + 1, 2 * (rest % 4) + 1]).astype(jnp.float32)
    first, second = jax.random.split(jax.random.fold_in(key, 12))
    spread = jnp.array([2.0, 1.0, 1.0], jnp.float32)[:, None]
    block_mid = centre + jax.random.uniform(first, (3, count), jnp.float32, -1.0, 1.0) * spread
    inner = jax.random.uniform(second, (3, count, BLOCK_SEGS), jnp.float32, -0.5, 0.5)
    return (block_mid[:, :, None] + inner).reshape(3, count * BLOCK_SEGS)


def draw_pairs(key, part):
    total = N_SLAB * N_DOM * MOST_BLOCK_PAIRS
    rows = jnp.arange(total, dtype=jnp.int32)
    owner = rows // MOST_BLOCK_PAIRS
    slabs = owner // N_DOM
    doms = owner % N_DOM
    kfirst, kslab, kdom, kblock = jax.random.split(jax.random.fold_in(key, 31), 4)
    first = owner * BLK_DEV + jax.random.randint(kfirst, (total,), 0, BLK_DEV)
    other_slab = jnp.clip(slabs + jax.random.randint(kslab, (total,), -1, 2), 0, N_SLAB - 1)
    other_dom = jnp.clip(doms + jax.random.randint(kdom, (total,), -1, 2), 0, N_DOM - 1)
    second = (other_slab * N_DOM + other_dom) * BLK_DEV + jax.random.randint(kblock, (total,), 0, BLK_DEV)
    spare_dom = jnp.where(doms < N_DOM - 1, doms + 1, doms - 1)
    spare = (slabs * N_DOM + spare_dom) * BLK_DEV + first % BLK_DEV
    second = jnp.where(second == first, spare, second)
    return jnp.stack([first, second], axis=1).astype(jnp.int32)


def draw_pair_count(key, part):
    device_list = N_SLAB * N_DOM
    heated_key, lowest_key = jax.random.split(jax.random.fold_in(key, 21))
    hot = jax.random.randint(heated_key, (N_SLAB,), 0, N_DOM)
    index = jnp.arange(device_list, dtype=jnp.int32)
    slabs = index // N_DOM
    doms = index % N_DOM
    lower_bound = jax.random.randint(lowest_key, (device_list,), MOST_BLOCK_PAIRS // 8, MOST_BLOCK_PAIRS // 2 + 1)
    return jnp.where(doms == hot[slabs], MOST_BLOCK_PAIRS, lower_bound).astype(jnp.int32)


def steps_of(stream_key, extent, shards, least, top_value):
    factor_of = 1.0
    for position, parts in shards:
        heights = jax.random.uniform(jax.random.fold_in(jax.random.fold_in(stream_key, 6), position), (parts,), jnp.float32, least / len(shards), top_value / len(shards))
        factor_of = factor_of * jnp.repeat(jnp.exp(heights), extent[position] // parts).reshape((-1,) + (1,) * (len(extent) - 1 - position))
    return factor_of


def bell_draw(rng, dims, scale, bound, cuts=(), kind=jnp.bfloat16):
    result = scale * jax.random.normal(rng, dims, jnp.float32)
    if cuts:
        result = result * steps_of(rng, dims, cuts, -0.22, 0.18)
    return jnp.clip(result, -bound, bound).astype(kind)


def setup_inputs(seed: int = 0) -> dict:
    seeds = jax.random.split(jax.random.key(seed), 7)
    positions = draw_positions(jax.random.fold_in(seeds[6], 71), 0)
    burgers = bell_draw(seeds[1], (3, SEGS), 1.0, 6.0, ((1, 32),), jnp.float32)
    mobility = jnp.clip(jnp.exp(math.log(2.0) - 1.3862944 * jax.random.uniform(seeds[2], (SEGS,), jnp.float32) ** steps_of(seeds[2], (SEGS,), ((0, 32),), -0.2, 0.2)), 0.5, 2.0)
    block_cells = draw_block_cells(jax.random.fold_in(seeds[6], 71), 0)
    pairs = draw_pairs(jax.random.fold_in(seeds[6], 71), 0)
    pair_count = draw_pair_count(jax.random.fold_in(seeds[6], 71), 0)
    return {"positions": positions, "burgers": burgers, "mobility": mobility, "block_cells": block_cells, "pairs": pairs, "pair_count": pair_count}


core_near = 0.25
core_far = 9.0
time_increment = 0.25
hi_prec = lax.Precision.HIGHEST

def centers(cells):
    whole = cells.astype(jnp.int32)
    slabs = whole // 16
    rest = whole % 16
    return jnp.stack([4 * slabs + 2, 2 * (rest // 4) + 1, 2 * (rest % 4) + 1]).astype(jnp.float32)

def block_moments(posit, burg, cells, ncells, width):
    nblk = cells.shape[0]
    offset = posit.reshape(3, nblk, width) - centers(cells)[:, :, None]
    vec = burg.reshape(3, nblk, width)
    first = (vec[:, None] * offset[None]).reshape(9, nblk, width)
    second = (vec[:, None, None] * offset[None, :, None] * offset[None, None, :]).reshape(27, nblk, width)
    rows = lax.optimization_barrier(jnp.sum(jnp.concatenate([vec, first, second], axis=0), axis=2))
    onehot = (cells[:, None] == jnp.arange(ncells, dtype=jnp.int32)[None, :]).astype(jnp.float32)
    return jnp.dot(rows, onehot, precision=hi_prec)

def far_field(posit, burg, moments):
    ncells = moments.shape[1]
    nblk = ncells // 64
    zeds = centers(jnp.arange(ncells, dtype=jnp.int32)).reshape(3, nblk, 64).transpose(1, 0, 2)
    mblk = moments.reshape(39, nblk, 64).transpose(1, 0, 2)

    def visit(acc, item):
        zpart, mpart = item
        r = posit[:, None, :] - zpart[:, :, None]
        sq = r[0] * r[0] + r[1] * r[1] + r[2] * r[2] + core_far
        inv3 = 1.0 / (sq * jnp.sqrt(sq))
        inv5 = inv3 / sq
        inv7 = inv5 / sq
        qzero = jnp.einsum('kc,kn->cn', mpart[0:3], burg, precision=hi_prec)
        qone = jnp.einsum('kac,kn->acn', mpart[3:12].reshape(3, 3, 64), burg, precision=hi_prec)
        qtwo = jnp.einsum('kabc,kn->abcn', mpart[12:39].reshape(3, 3, 3, 64), burg, precision=hi_prec)
        qone_r = lax.optimization_barrier(jnp.sum(qone * r, axis=0))
        qtwo_r = lax.optimization_barrier(jnp.sum(qtwo * r[None], axis=1))
        rqr = lax.optimization_barrier(jnp.sum(r * qtwo_r, axis=0))
        trace = qtwo[0, 0] + qtwo[1, 1] + qtwo[2, 2]
        scal = qzero * inv3 + 3.0 * qone_r * inv5 - 1.5 * trace * inv5 + 7.5 * rqr * inv7
        force = r * scal[None] - qone * inv3[None] - 3.0 * qtwo_r * inv5[None]
        return (acc + lax.optimization_barrier(jnp.sum(force, axis=1)), None)
    start = jnp.zeros(posit.shape, jnp.float32)
    total, unused = lax.scan(visit, start, (zeds, mblk))
    return total

def pair_forces(pos_a, bur_a, pos_b, bur_b, weight):
    r = pos_a[:, :, :, None] - pos_b[:, :, None, :]
    sq = r[0] * r[0] + r[1] * r[1] + r[2] * r[2]
    near_s = sq + core_near
    far_s = sq + core_far
    kern = 1.0 / (near_s * jnp.sqrt(near_s)) - 1.0 / (far_s * jnp.sqrt(far_s))
    coef = lax.optimization_barrier(jnp.sum(bur_a[:, :, :, None] * bur_b[:, :, None, :], axis=0))
    wgt = weight[:, None, None] * coef * kern
    wr = wgt[None] * r
    return (lax.optimization_barrier(jnp.sum(wr, axis=3)), -lax.optimization_barrier(jnp.sum(wr, axis=2)))

def reference(positions, burgers, mobility, block_cells, pairs, pair_count):
    device_list = N_SLAB * N_DOM
    width = BLOCK_SEGS
    per_dev = BLK_DEV * BLOCK_SEGS
    far_scale = math.sqrt(CELLS / SEGS)

    def speed(posit):
        moments = block_moments(posit, burgers, block_cells, CELLS, width)
        pdev = posit.reshape(3, device_list, per_dev).transpose(1, 0, 2)
        bdev = burgers.reshape(3, device_list, per_dev).transpose(1, 0, 2)
        far = lax.map(lambda item: far_field(item[0], item[1], moments), (pdev, bdev))
        far = far.transpose(1, 0, 2).reshape(3, -1)
        pblk = posit.reshape(3, BLOCKS, width)
        bblk = burgers.reshape(3, BLOCKS, width)

        def visit(acc, item):
            plist, count = item
            weight = (jnp.arange(MOST_BLOCK_PAIRS, dtype=jnp.int32) < count).astype(jnp.float32)
            first = plist[:, 0]
            second = plist[:, 1]
            force_a, force_b = pair_forces(pblk[:, first], bblk[:, first], pblk[:, second], bblk[:, second], weight)
            return (acc.at[:, first].add(force_a).at[:, second].add(force_b), None)
        start = jnp.zeros((3, BLOCKS, width), jnp.float32)
        near, unused = lax.scan(visit, start, (pairs.reshape(device_list, MOST_BLOCK_PAIRS, 2), pair_count))
        return mobility[None, :] * (far_scale * far + near.reshape(3, -1))
    first_v = speed(positions)
    second_v = speed(positions + time_increment * first_v)
    total = first_v + second_v
    return (positions + 0.5 * time_increment * total, 0.5 * total)
```

```python
import functools
import math

import jax
import jax.numpy as jnp
from jax import lax
from jax.experimental import pallas as pl
from jax.experimental.pallas import tpu as pltpu
from jax.sharding import PartitionSpec as P

LANES = 128
SUB = 8
CORE_NEAR = 0.25
CORE_FAR = 9.0
TIME_INCREMENT = 0.25
EXACT = lax.Precision.HIGHEST
VMEM = pl.BlockSpec(memory_space=pltpu.VMEM)
SMEM = pl.BlockSpec(memory_space=pltpu.SMEM)
PARAMS = pltpu.CompilerParams(vmem_limit_bytes=24 * 1024 * 1024)
SYM = ((0, 0), (0, 1), (0, 2), (1, 1), (1, 2), (2, 2))
MOMS = 3 + 9 + 18


def dot_lanes(a, b, precision=EXACT):
    return lax.dot_general(
        a, b, (((1,), (1,)), ((), ())), precision=precision, preferred_element_type=jnp.float32
    )


def center_of(cell):
    slab = jnp.floor(cell * 0.0625)
    rest = cell - 16.0 * slab
    row = jnp.floor(rest * 0.25)
    col = rest - 4.0 * row
    return (4.0 * slab + 2.0, 2.0 * row + 1.0, 2.0 * col + 1.0)


def column_of(values, like):
    index = lax.broadcasted_iota(jnp.int32, like, 0)
    out = jnp.full(like, values[-1], jnp.float32)
    for j, value in enumerate(values[:-1]):
        out = jnp.where(index == j, value, out)
    return out


def moment_row(pos, bur, cells_ref, stack_ref):
    nblk = pos[0].shape[0]
    cell = column_of([cells_ref[b].astype(jnp.float32) for b in range(nblk)], pos[0].shape)
    z = center_of(cell)
    d = [pos[k] - z[k] for k in range(3)]
    dd = [d[a] * d[e] for a, e in SYM]
    stack_ref[...] = jnp.zeros_like(stack_ref)
    m = 0
    for k in range(3):
        stack_ref[m * nblk : (m + 1) * nblk, :] = bur[k]
        m += 1
    for k in range(3):
        for a in range(3):
            stack_ref[m * nblk : (m + 1) * nblk, :] = bur[k] * d[a]
            m += 1
    for k in range(3):
        for j in range(6):
            stack_ref[m * nblk : (m + 1) * nblk, :] = bur[k] * dd[j]
            m += 1
    sums = dot_lanes(jnp.ones((SUB, LANES), jnp.float32), stack_ref[...])[0:1, :]
    lane = lax.broadcasted_iota(jnp.int32, (1, LANES), 1)
    for b in range(nblk):
        sums = jnp.where(lane == MOMS * nblk + b, cells_ref[b].astype(jnp.float32), sums)
    return sums


def spread(out_ref, value):
    count = out_ref.shape[0]

    def put(d, carry):
        out_ref[d] = value
        return carry

    lax.fori_loop(0, count, put, 0, unroll=math.gcd(count, 32))


def first_kernel(cells_ref, count_ref, pos_ref, bur_ref, pairs_ref, out_ref, stack_ref, load_ref, ids_ref):
    nblk = cells_ref.shape[0]
    slots = pairs_ref.shape[0]
    pos, bur = [], []
    for k in range(3):
        for b in range(nblk):
            load_ref[k * nblk + b : k * nblk + b + 1, :] = pos_ref[k : k + 1, b * LANES : (b + 1) * LANES]
            load_ref[(3 + k) * nblk + b : (3 + k) * nblk + b + 1, :] = bur_ref[
                k : k + 1, b * LANES : (b + 1) * LANES
            ]
    for k in range(3):
        pos.append(load_ref[k * nblk : (k + 1) * nblk, :])
        bur.append(load_ref[(3 + k) * nblk : (4 + k) * nblk, :])
    base = 6 * nblk
    lane = lax.broadcasted_iota(jnp.int32, (slots, LANES), 1)
    row = lax.broadcasted_iota(jnp.int32, (slots, LANES), 0)
    ids = jnp.where(lane < slots, pairs_ref[:, 0:1], pairs_ref[:, 1:2])
    hit = (lane == row) | (lane == row + slots)
    listed = jnp.sum(jnp.where(hit, ids, 0), axis=0, keepdims=True)
    slot = lax.broadcasted_iota(jnp.int32, (1, LANES), 1)
    slot = jnp.where(slot < slots, slot, slot - slots)
    listed = jnp.where(slot < count_ref[0], listed, -1).astype(jnp.float32)
    load_ref[base : base + 1, :] = listed
    load_ref[base + 1 : base + 2, :] = moment_row(pos, bur, cells_ref, stack_ref)
    rows = base + 2
    for r in range(rows):
        ids_ref[:, r * LANES : (r + 1) * LANES] = load_ref[r : r + 1, :]
    spread(out_ref, ids_ref[...])


def far_into(pos_row, bur_row, mom_ref, far_ref, nblk, ndev):
    def visit(g, carry):
        block = mom_ref[pl.ds(g * SUB, SUB), :]
        zall = center_of(block)

        def wide(x, lane):
            return jnp.broadcast_to(x[:, lane : lane + 1], (SUB, LANES))

        acc = list(carry)
        for b in range(nblk):
            mom = [wide(block, m * nblk + b) for m in range(MOMS)]
            z = [wide(zall[k], MOMS * nblk + b) for k in range(3)]
            for t in range(nblk):
                p = [pos_row(k, t) for k in range(3)]
                c = [bur_row(k, t) for k in range(3)]
                q0 = c[0] * mom[0] + c[1] * mom[1] + c[2] * mom[2]
                q1 = [c[0] * mom[3 + a] + c[1] * mom[6 + a] + c[2] * mom[9 + a] for a in range(3)]
                q2 = [c[0] * mom[12 + j] + c[1] * mom[18 + j] + c[2] * mom[24 + j] for j in range(6)]
                r = [p[k] - z[k] for k in range(3)]
                sq = r[0] * r[0] + r[1] * r[1] + (r[2] * r[2] + CORE_FAR)
                inv = lax.rsqrt(sq)
                inv2 = inv * inv
                inv3 = inv2 * inv
                u = [
                    q2[0] * r[0] + q2[1] * r[1] + q2[2] * r[2],
                    q2[1] * r[0] + q2[3] * r[1] + q2[4] * r[2],
                    q2[2] * r[0] + q2[4] * r[1] + q2[5] * r[2],
                ]
                q1r = q1[0] * r[0] + q1[1] * r[1] + q1[2] * r[2]
                rqr = u[0] * r[0] + u[1] * r[1] + u[2] * r[2]
                trace = q2[0] + q2[3] + q2[5]
                inner = (3.0 * q1r - 1.5 * trace) + (7.5 * rqr) * inv2
                scal = q0 + inner * inv2
                three = 3.0 * inv2
                for k in range(3):
                    f = (r[k] * scal - (q1[k] + three * u[k])) * inv3
                    acc[k * nblk + t] = acc[k * nblk + t] + f
        return tuple(acc)

    zero = jnp.zeros((SUB, LANES), jnp.float32)
    total = lax.fori_loop(0, ndev // SUB, visit, (zero,) * (3 * nblk))
    for j in range(3 * nblk):
        far_ref[j : j + 1, :] = jnp.sum(total[j], axis=0, keepdims=True)


def near_into(pos_of, bur_of, own_ref, list_ref, mult_ref, used_ref, acc_ref, near_ref, nblk):
    for a in range(nblk):
        acc_ref[...] = jnp.zeros_like(acc_ref)

        def visit(n, carry):
            g = list_ref[a, n]
            mult = mult_ref[a, n]
            p = [jnp.broadcast_to(pos_of(g, k), (SUB, LANES)) for k in range(3)]
            c = [jnp.broadcast_to(bur_of(g, k) * mult, (SUB, LANES)) for k in range(3)]
            for t in range(LANES // SUB):
                rows = slice(t * SUB, (t + 1) * SUB)
                r = [own_ref[a, k, rows, :] - p[k] for k in range(3)]
                sq = r[0] * r[0] + r[1] * r[1] + (r[2] * r[2] + CORE_NEAR)
                u = lax.rsqrt(sq)
                w = lax.rsqrt(sq + (CORE_FAR - CORE_NEAR))
                kern = u * u * u - w * w * w
                coef = (
                    own_ref[a, 3, rows, :] * c[0]
                    + own_ref[a, 4, rows, :] * c[1]
                    + own_ref[a, 5, rows, :] * c[2]
                )
                wgt = coef * kern
                for k in range(3):
                    acc_ref[k, rows, :] = acc_ref[k, rows, :] + wgt * r[k]
            return carry

        lax.fori_loop(0, used_ref[a], visit, 0)
        ones = jnp.ones((SUB, LANES), jnp.float32)
        for k in range(3):
            near_ref[k * nblk + a : k * nblk + a + 1, :] = dot_lanes(ones, acc_ref[k])[0:1, :]


def widen_own(row_of, own_ref, nblk, kinds):
    for a in range(nblk):
        for k in kinds:
            own_ref[a, k] = jnp.transpose(jnp.broadcast_to(row_of(k, a), (LANES, LANES)))


def build_lists(got_ref, rows, nblk, my_slab, my_dom, n_slab, n_dom, count_ref, count_smem, sem, list_ref, mult_ref, used_ref):
    base = 6 * nblk
    wide = 9 * nblk
    high = -(-wide // SUB) * SUB
    index = lax.broadcasted_iota(jnp.int32, (high, LANES), 0)
    gid = jnp.full((high, LANES), -2.0, jnp.float32)
    for k in range(9):
        ds, dd = k // 3 - 1, k % 3 - 1
        s, e = my_slab + ds, my_dom + dd
        inside = (s >= 0) & (s < n_slab) & (e >= 0) & (e < n_dom)
        first = jnp.where(inside, (s * n_dom + e) * nblk - k * nblk, -100000)
        here = (index >= k * nblk) & (index < (k + 1) * nblk)
        gid = jnp.where(here, (index + first).astype(jnp.float32), gid)
    own = (my_slab * n_dom + my_dom) * nblk
    small = lax.broadcasted_iota(jnp.int32, (SUB, LANES), 0)
    mine = jnp.where(small < nblk, small + own, -3).astype(jnp.float32)
    total = jnp.zeros((SUB, high), jnp.float32)
    for k in range(9):
        ds, dd = k // 3 - 1, k % 3 - 1
        s, e = my_slab + ds, my_dom + dd
        inside = (s >= 0) & (s < n_slab) & (e >= 0) & (e < n_dom)
        dev = jnp.clip(s, 0, n_slab - 1) * n_dom + jnp.clip(e, 0, n_dom - 1)
        row = got_ref[dev * rows + base]
        row = jnp.where(inside, row, -1.0)
        other = pltpu.roll(row, LANES // 2, 1)
        left = (mine == row).astype(jnp.float32)
        right = (gid == other).astype(jnp.float32)
        total = total + dot_lanes(left, right, None)
    count_ref[:, 0:high] = total
    copy = pltpu.make_async_copy(count_ref, count_smem, sem)
    copy.start()
    copy.wait()

    def visit(w, carry):
        k = w // nblk
        s = my_slab + k // 3 - 1
        e = my_dom + k % 3 - 1
        g = (s * n_dom + e) * nblk + w % nblk
        out = []
        for a in range(nblk):
            c = count_smem[a, w]
            list_ref[a, carry[a]] = g
            mult_ref[a, carry[a]] = c
            out.append(carry[a] + jnp.where(c > 0.5, 1, 0).astype(jnp.int32))
        return tuple(out)

    ends = lax.fori_loop(0, wide, visit, (jnp.int32(0),) * nblk)
    for a in range(nblk):
        used_ref[a] = ends[a]


def gather_moments(got_ref, rows, mom_ref, ndev):
    def take(d, carry):
        mom_ref[pl.ds(d, 1), :] = got_ref[d * rows + rows - 1]
        return carry

    lax.fori_loop(0, ndev, take, 0, unroll=math.gcd(ndev, 32))


def second_kernel(
    n_slab, n_dom, far_scale,
    cells_ref, mob_ref, got_ref,
    out_ref, vel_ref, list_ref, mult_ref, used_ref,
    stack_ref, own_ref, acc_ref, near_ref, far_ref, mom_ref, count_ref, next_ref, flat_ref, count_smem, sem,
):
    nblk = cells_ref.shape[0]
    ndev = n_slab * n_dom
    rows = got_ref.shape[0] // ndev
    my_slab, my_dom = lax.axis_index("slab"), lax.axis_index("dom")
    me = my_slab * n_dom + my_dom

    def own_row(k, b):
        return got_ref[me * rows + k * nblk + b]

    def block_row(g, k):
        return got_ref[(g // nblk) * rows + g % nblk + k * nblk]

    build_lists(
        got_ref, rows, nblk, my_slab, my_dom, n_slab, n_dom,
        count_ref, count_smem, sem, list_ref, mult_ref, used_ref,
    )
    gather_moments(got_ref, rows, mom_ref, ndev)
    widen_own(own_row, own_ref, nblk, range(6))
    near_into(
        block_row, lambda g, k: block_row(g, k + 3), own_ref, list_ref, mult_ref, used_ref,
        acc_ref, near_ref, nblk,
    )
    far_into(own_row, lambda k, b: own_row(k + 3, b), mom_ref, far_ref, nblk, ndev)
    pos, bur = [], []
    for k in range(3):
        here = slice(k * nblk, (k + 1) * nblk)
        vel = mob_ref[...] * (far_scale * far_ref[here, :] + near_ref[here, :])
        vel_ref[here, :] = vel
        for b in range(nblk):
            next_ref[k * nblk + b : k * nblk + b + 1, :] = own_row(k, b)
            next_ref[(3 + k) * nblk + b : (3 + k) * nblk + b + 1, :] = own_row(3 + k, b)
        moved = next_ref[here, :] + TIME_INCREMENT * vel
        next_ref[here, :] = moved
        pos.append(moved)
        bur.append(next_ref[(3 + k) * nblk : (4 + k) * nblk, :])
    last = moment_row(pos, bur, cells_ref, stack_ref)
    for r in range(3 * nblk):
        flat_ref[:, r * LANES : (r + 1) * LANES] = next_ref[r : r + 1, :]
    flat_ref[:, 3 * nblk * LANES :] = last
    spread(out_ref, flat_ref[...])


def third_kernel(
    n_slab, n_dom, far_scale,
    mob_ref, pos_ref, vel_ref, old_ref, got_ref, list_ref, mult_ref, used_ref,
    moved_ref, velocity_ref,
    own_ref, acc_ref, near_ref, far_ref, mom_ref,
):
    nblk = mob_ref.shape[0]
    ndev = n_slab * n_dom
    rows = got_ref.shape[0] // ndev
    old_rows = old_ref.shape[0] // ndev
    me = lax.axis_index("slab") * n_dom + lax.axis_index("dom")

    def row_of(k, b):
        if k < 3:
            return got_ref[me * rows + k * nblk + b]
        return old_ref[me * old_rows + k * nblk + b]

    gather_moments(got_ref, rows, mom_ref, ndev)
    widen_own(row_of, own_ref, nblk, range(6))
    near_into(
        lambda g, k: got_ref[(g // nblk) * rows + g % nblk + k * nblk],
        lambda g, k: old_ref[(g // nblk) * old_rows + g % nblk + (3 + k) * nblk],
        own_ref, list_ref, mult_ref, used_ref, acc_ref, near_ref, nblk,
    )
    far_into(row_of, lambda k, b: row_of(k + 3, b), mom_ref, far_ref, nblk, ndev)
    for k in range(3):
        here = slice(k * nblk, (k + 1) * nblk)
        vel = mob_ref[...] * (far_scale * far_ref[here, :] + near_ref[here, :])
        near_ref[here, :] = 0.5 * (vel_ref[here, :] + vel)
        for b in range(nblk):
            lanes = slice(b * LANES, (b + 1) * LANES)
            mean = near_ref[k * nblk + b : k * nblk + b + 1, :]
            velocity_ref[k : k + 1, lanes] = mean
            moved_ref[k : k + 1, lanes] = pos_ref[k : k + 1, lanes] + TIME_INCREMENT * mean


def body(positions, burgers, mobility, block_cells, pairs, pair_count):
    f32 = jnp.float32
    segs = positions.shape[1]
    nblk = block_cells.shape[0]
    n_slab, n_dom = lax.axis_size("slab"), lax.axis_size("dom")
    ndev = n_slab * n_dom
    far_scale = math.sqrt(16 * n_slab / (segs * ndev))
    rows, rows2 = 6 * nblk + 2, 3 * nblk + 1
    wide = 9 * nblk
    mob = mobility.reshape(nblk, LANES)
    high = -(-(3 * nblk) // SUB) * SUB
    scratch = [
        pltpu.VMEM((nblk, 6, LANES, LANES), f32),
        pltpu.VMEM((3, LANES, LANES), f32),
        pltpu.VMEM((high, LANES), f32),
        pltpu.VMEM((high, LANES), f32),
        pltpu.VMEM((ndev, LANES), f32),
    ]
    load = pl.pallas_call(
        first_kernel,
        out_shape=jax.ShapeDtypeStruct((ndev, 1, rows * LANES), f32),
        in_specs=[SMEM, SMEM, VMEM, VMEM, VMEM],
        out_specs=VMEM,
        scratch_shapes=[
            pltpu.VMEM((LANES, LANES), f32),
            pltpu.VMEM((-(-rows // SUB) * SUB, LANES), f32),
            pltpu.VMEM((1, rows * LANES), f32),
        ],
        compiler_params=PARAMS,
        name="pack",
    )(block_cells, pair_count, positions, burgers, pairs)
    got = lax.all_to_all(load, ("slab", "dom"), 0, 0, tiled=True).reshape(ndev * rows, 1, LANES)
    load2, vel, lists, mult, used = pl.pallas_call(
        functools.partial(second_kernel, n_slab, n_dom, far_scale),
        out_shape=(
            jax.ShapeDtypeStruct((ndev, 1, rows2 * LANES), f32),
            jax.ShapeDtypeStruct((3 * nblk, LANES), f32),
            jax.ShapeDtypeStruct((nblk, wide + 1), jnp.int32),
            jax.ShapeDtypeStruct((nblk, wide + 1), f32),
            jax.ShapeDtypeStruct((nblk,), jnp.int32),
        ),
        in_specs=[SMEM, VMEM, VMEM],
        out_specs=(VMEM, VMEM, SMEM, SMEM, SMEM),
        scratch_shapes=[pltpu.VMEM((LANES, LANES), f32)]
        + scratch
        + [
            pltpu.VMEM((SUB, LANES), f32),
            pltpu.VMEM((6 * nblk, LANES), f32),
            pltpu.VMEM((1, rows2 * LANES), f32),
            pltpu.SMEM((SUB, LANES), f32),
            pltpu.SemaphoreType.DMA(()),
        ],
        compiler_params=PARAMS,
        name="step_one",
    )(block_cells, mob, got)
    got2 = lax.all_to_all(load2, ("slab", "dom"), 0, 0, tiled=True).reshape(ndev * rows2, 1, LANES)
    return pl.pallas_call(
        functools.partial(third_kernel, n_slab, n_dom, far_scale),
        out_shape=(jax.ShapeDtypeStruct((3, segs), f32),) * 2,
        in_specs=[VMEM, VMEM, VMEM, VMEM, VMEM, SMEM, SMEM, SMEM],
        out_specs=(VMEM, VMEM),
        scratch_shapes=scratch,
        compiler_params=PARAMS,
        name="step_two",
    )(mob, positions, vel, got, got2, lists, mult, used)


def solution(mesh):
    placed = (
        P(None, ("slab", "dom")),
        P(None, ("slab", "dom")),
        P(("slab", "dom")),
        P(("slab", "dom")),
        P(("slab", "dom"), None),
        P(("slab", "dom")),
    )
    return jax.shard_map(
        body,
        mesh=mesh,
        in_specs=placed,
        out_specs=(P(None, ("slab", "dom")), P(None, ("slab", "dom"))),
        check_vma=False,
    )
```

```python
import functools
import math

import jax
import jax.numpy as jnp
from jax import lax
from jax.experimental import pallas as pl
from jax.experimental.pallas import tpu as pltpu
from jax.sharding import PartitionSpec as P

LANES = 128
SUB = 8
CORE_NEAR = 0.25
CORE_FAR = 9.0
TIME_INCREMENT = 0.25
EXACT = lax.Precision.HIGHEST
VMEM = pl.BlockSpec(memory_space=pltpu.VMEM)
SMEM = pl.BlockSpec(memory_space=pltpu.SMEM)
PARAMS = pltpu.CompilerParams(vmem_limit_bytes=24 * 1024 * 1024)
SYM = ((0, 0), (0, 1), (0, 2), (1, 1), (1, 2), (2, 2))
MOMS = 3 + 9 + 18


def dot_lanes(a, b, precision=EXACT):
    return lax.dot_general(
        a, b, (((1,), (1,)), ((), ())), precision=precision, preferred_element_type=jnp.float32
    )


def center_of(cell):
    slab = jnp.floor(cell * 0.0625)
    rest = cell - 16.0 * slab
    row = jnp.floor(rest * 0.25)
    col = rest - 4.0 * row
    return (4.0 * slab + 2.0, 2.0 * row + 1.0, 2.0 * col + 1.0)


def column_of(values, like):
    index = lax.broadcasted_iota(jnp.int32, like, 0)
    out = jnp.full(like, values[-1], jnp.float32)
    for j, value in enumerate(values[:-1]):
        out = jnp.where(index == j, value, out)
    return out


def moment_row(pos, bur, cells_ref, stack_ref):
    nblk = pos[0].shape[0]
    cell = column_of([cells_ref[b].astype(jnp.float32) for b in range(nblk)], pos[0].shape)
    z = center_of(cell)
    d = [pos[k] - z[k] for k in range(3)]
    dd = [d[a] * d[e] for a, e in SYM]
    stack_ref[...] = jnp.zeros_like(stack_ref)
    m = 0
    for k in range(3):
        stack_ref[m * nblk : (m + 1) * nblk, :] = bur[k]
        m += 1
    for k in range(3):
        for a in range(3):
            stack_ref[m * nblk : (m + 1) * nblk, :] = bur[k] * d[a]
            m += 1
    for k in range(3):
        for j in range(6):
            stack_ref[m * nblk : (m + 1) * nblk, :] = bur[k] * dd[j]
            m += 1
    sums = dot_lanes(jnp.ones((SUB, LANES), jnp.float32), stack_ref[...])[0:1, :]
    lane = lax.broadcasted_iota(jnp.int32, (1, LANES), 1)
    for b in range(nblk):
        sums = jnp.where(lane == MOMS * nblk + b, cells_ref[b].astype(jnp.float32), sums)
    return sums


def spread(out_ref, value):
    count = out_ref.shape[0]

    def put(d, carry):
        out_ref[d] = value
        return carry

    lax.fori_loop(0, count, put, 0, unroll=math.gcd(count, 32))


def first_kernel(
    cells_ref, count_ref, pos_ref, bur_ref, pairs_ref, mob_in_ref, out_ref, mob_ref, stack_ref, load_ref, ids_ref
):
    mob_ref[...] = mob_in_ref[...]
    nblk = cells_ref.shape[0]
    slots = pairs_ref.shape[0]
    pos, bur = [], []
    for k in range(3):
        for b in range(nblk):
            load_ref[k * nblk + b : k * nblk + b + 1, :] = pos_ref[k : k + 1, b * LANES : (b + 1) * LANES]
            load_ref[(3 + k) * nblk + b : (3 + k) * nblk + b + 1, :] = bur_ref[
                k : k + 1, b * LANES : (b + 1) * LANES
            ]
    for k in range(3):
        pos.append(load_ref[k * nblk : (k + 1) * nblk, :])
        bur.append(load_ref[(3 + k) * nblk : (4 + k) * nblk, :])
    base = 6 * nblk
    lane = lax.broadcasted_iota(jnp.int32, (slots, LANES), 1)
    row = lax.broadcasted_iota(jnp.int32, (slots, LANES), 0)
    ids = jnp.where(lane < slots, pairs_ref[:, 0:1], pairs_ref[:, 1:2])
    hit = (lane == row) | (lane == row + slots)
    listed = jnp.sum(jnp.where(hit, ids, 0), axis=0, keepdims=True)
    slot = lax.broadcasted_iota(jnp.int32, (1, LANES), 1)
    slot = jnp.where(slot < slots, slot, slot - slots)
    listed = jnp.where(slot < count_ref[0], listed, -1).astype(jnp.float32)
    load_ref[base : base + 1, :] = listed
    load_ref[base + 1 : base + 2, :] = moment_row(pos, bur, cells_ref, stack_ref)
    rows = base + 2
    for r in range(rows):
        ids_ref[:, r * LANES : (r + 1) * LANES] = load_ref[r : r + 1, :]
    spread(out_ref, ids_ref[...])


def far_into(own_ref, mom_ref, center_ref, acc_ref, nblk, chunks):
    def visit(c, a, first):
        for t in range(LANES // SUB):
            rows = slice(t * SUB, (t + 1) * SUB)

            def mom(m):
                return mom_ref[c, m * nblk : m * nblk + 1, :]

            b = [own_ref[a, 3 + k, rows, :] for k in range(3)]
            r = [own_ref[a, k, rows, :] - center_ref[c, k : k + 1, :] for k in range(3)]
            sq = r[0] * r[0] + r[1] * r[1] + (r[2] * r[2] + CORE_FAR)
            inv = lax.rsqrt(sq)
            inv2 = inv * inv
            inv3 = inv2 * inv
            q0 = b[0] * mom(0) + b[1] * mom(1) + b[2] * mom(2)
            q1 = [b[0] * mom(3 + e) + b[1] * mom(6 + e) + b[2] * mom(9 + e) for e in range(3)]
            q2 = [b[0] * mom(12 + j) + b[1] * mom(18 + j) + b[2] * mom(24 + j) for j in range(6)]
            u = [
                q2[0] * r[0] + q2[1] * r[1] + q2[2] * r[2],
                q2[1] * r[0] + q2[3] * r[1] + q2[4] * r[2],
                q2[2] * r[0] + q2[4] * r[1] + q2[5] * r[2],
            ]
            q1r = q1[0] * r[0] + q1[1] * r[1] + q1[2] * r[2]
            rqr = u[0] * r[0] + u[1] * r[1] + u[2] * r[2]
            trace = q2[0] + q2[3] + q2[5]
            inner = (3.0 * q1r - 0.5 * trace) + (2.5 * rqr) * inv2
            scal = q0 + inner * inv2
            for k in range(3):
                f = (r[k] * scal - (q1[k] + inv2 * u[k])) * inv3
                acc_ref[a, k, rows, :] = f if first else acc_ref[a, k, rows, :] + f

    def start(a, carry):
        visit(0, a, True)
        return carry

    def more(n, carry):
        visit(1 + n // nblk, n % nblk, False)
        return carry

    lax.fori_loop(0, nblk, start, 0)
    if chunks > 1:
        lax.fori_loop(0, nblk * (chunks - 1), more, 0)


def near_into(row_pos, coef_of, own_ref, used_of, acc_ref, nblk):
    for a in range(nblk):

        def visit(n, carry):
            pair = (2 * n, 2 * n + 1)
            p = [[jnp.broadcast_to(row_pos(a, e, k), (SUB, LANES)) for k in range(3)] for e in pair]
            weigh = [coef_of(a, e) for e in pair]
            for t in range(LANES // SUB):
                rows = slice(t * SUB, (t + 1) * SUB)
                own = [own_ref[a, k, rows, :] for k in range(3)]
                f = []
                for j in range(2):
                    r = [own[k] - p[j][k] for k in range(3)]
                    sq = r[0] * r[0] + r[1] * r[1] + (r[2] * r[2] + CORE_NEAR)
                    u = lax.rsqrt(sq)
                    w = lax.rsqrt(sq + (CORE_FAR - CORE_NEAR))
                    wgt = weigh[j](t, rows) * (u * u * u - w * w * w)
                    f.append([wgt * r[k] for k in range(3)])
                for k in range(3):
                    acc_ref[a, k, rows, :] = acc_ref[a, k, rows, :] + (f[0][k] + f[1][k])
            return carry

        lax.fori_loop(0, (used_of(a) + 1) // 2, visit, 0)


def sum_lanes(acc_ref, force_ref, nblk):
    lane = lax.broadcasted_iota(jnp.int32, (SUB, LANES), 1)
    offset = lane - lax.broadcasted_iota(jnp.int32, (SUB, LANES), 0)
    for a in range(nblk):
        for k in range(3):
            out = jnp.zeros((SUB, LANES), jnp.float32)
            for t in range(LANES // SUB):
                total = jnp.sum(acc_ref[a, k, t * SUB : (t + 1) * SUB, :], axis=1, keepdims=True)
                out = jnp.where(offset == t * SUB, total, out)
            force_ref[k * nblk + a : k * nblk + a + 1, :] = jnp.sum(out, axis=0, keepdims=True)


def widen_own(row_of, own_ref, nblk, kinds):
    for a in range(nblk):
        for k in kinds:
            own_ref[a, k] = jnp.transpose(jnp.broadcast_to(row_of(k, a), (LANES, LANES)))


def window_ids(index, my_slab, my_dom, n_slab, n_dom, nblk):
    ids = jnp.full(index.shape, -2.0, jnp.float32)
    for k in range(9):
        s, e = my_slab + k // 3 - 1, my_dom + k % 3 - 1
        inside = (s >= 0) & (s < n_slab) & (e >= 0) & (e < n_dom)
        first = jnp.where(inside, (s * n_dom + e) * nblk - k * nblk, -100000)
        here = (index >= k * nblk) & (index < (k + 1) * nblk)
        ids = jnp.where(here, (index + first).astype(jnp.float32), ids)
    return ids


def build_lists(got_ref, rows, nblk, my_slab, my_dom, n_slab, n_dom, count_ref, list_ref, mult_ref):
    base = 6 * nblk
    high = -(-9 * nblk // SUB) * SUB
    place = (my_slab, my_dom, n_slab, n_dom, nblk)
    gid = window_ids(lax.broadcasted_iota(jnp.int32, (high, LANES), 0), *place)
    own = (my_slab * n_dom + my_dom) * nblk
    sub = lax.broadcasted_iota(jnp.int32, (SUB, LANES), 0)
    lane = lax.broadcasted_iota(jnp.int32, (SUB, LANES), 1)
    mine = jnp.where(sub < nblk, sub + own, -3).astype(jnp.float32)
    total = jnp.zeros((SUB, high), jnp.float32)
    for k in range(9):
        s, e = my_slab + k // 3 - 1, my_dom + k % 3 - 1
        inside = (s >= 0) & (s < n_slab) & (e >= 0) & (e < n_dom)
        dev = jnp.clip(s, 0, n_slab - 1) * n_dom + jnp.clip(e, 0, n_dom - 1)
        row = jnp.where(inside, got_ref[dev * rows + base], -1.0)
        other = pltpu.roll(row, LANES // 2, 1)
        left = (mine == row).astype(jnp.float32)
        right = (gid == other).astype(jnp.float32)
        total = total + dot_lanes(left, right, None)
    count_ref[...] = jnp.zeros_like(count_ref)
    count_ref[:, 0:high] = total
    count = count_ref[...]
    met = jnp.where(count > 0.5, 1.0, 0.0)
    before = lax.broadcasted_iota(jnp.int32, (LANES, LANES), 1) < lax.broadcasted_iota(
        jnp.int32, (LANES, LANES), 0
    )
    rank = dot_lanes(met, before.astype(jnp.float32), None)
    used = jnp.sum(met, axis=1, keepdims=True).astype(jnp.int32)
    list_ref[...] = jnp.where(lane == LANES - 1, used, 0)
    mult_ref[...] = jnp.zeros_like(mult_ref)
    line = window_ids(lane, *place)
    spot = lax.broadcasted_iota(jnp.int32, (high, LANES), 0).astype(jnp.float32)
    for a in range(nblk):
        pick = (rank[a : a + 1, :] == spot) & (met[a : a + 1, :] > 0.5)
        what = jnp.where(sub == 0, line, jnp.where(sub == 1, count[a : a + 1, :], 0.0))
        out = dot_lanes(what, pick.astype(jnp.float32))
        list_ref[a : a + 1, 0:high] = (out[0:1, :] + 0.5).astype(jnp.int32)
        mult_ref[a : a + 1, 0:high] = out[1:2, :]


def gather_moments(got_ref, rows, mom_ref, center_ref, take_ref, nblk, ndev, far_scale):
    width = LANES // nblk
    for c in range(ndev // width):

        def take(d, carry):
            take_ref[pl.ds(d, 1), :] = got_ref[(c * width + d) * rows + rows - 1]
            return carry

        lax.fori_loop(0, width, take, 0, unroll=True)
        block = take_ref[...]
        turned = [block] + [pltpu.roll(block, LANES - b, 1) for b in range(1, nblk)]
        flat = jnp.transpose(jnp.concatenate(turned, axis=0))
        z = center_of(flat[MOMS * nblk : MOMS * nblk + 1, :])
        for k in range(3):
            center_ref[c, k : k + 1, :] = z[k]
        row = lax.broadcasted_iota(jnp.int32, (LANES, LANES), 0)
        mom_ref[c] = flat * jnp.where(row < 12 * nblk, far_scale, 3.0 * far_scale)


def second_kernel(
    n_slab, n_dom, far_scale,
    cells_ref, mob_ref, got_ref,
    out_ref, vel_ref, list_ref, coef_ref,
    stack_ref, own_ref, acc_ref, force_ref, mom_ref, center_ref, take_ref,
    count_ref, mult_ref, next_ref, flat_ref, list_smem, mult_smem, sem,
):
    nblk = cells_ref.shape[0]
    ndev = n_slab * n_dom
    rows = got_ref.shape[0] // ndev
    each = coef_ref.shape[0] // nblk
    my_slab, my_dom = lax.axis_index("slab"), lax.axis_index("dom")
    me = my_slab * n_dom + my_dom

    def own_row(k, b):
        return got_ref[me * rows + k * nblk + b]

    def block_row(g, k):
        return got_ref[(g // nblk) * rows + g % nblk + k * nblk]

    def coef_of(a, e):
        g, mult = list_smem[a, e], mult_smem[a, e]
        c = [jnp.broadcast_to(block_row(g, 3 + k) * mult, (SUB, LANES)) for k in range(3)]

        def tile(t, rows):
            value = (
                own_ref[a, 3, rows, :] * c[0] + own_ref[a, 4, rows, :] * c[1] + own_ref[a, 5, rows, :] * c[2]
            )
            coef_ref[a * each + e, rows, :] = value
            return value

        return tile

    build_lists(got_ref, rows, nblk, my_slab, my_dom, n_slab, n_dom, count_ref, list_ref, mult_ref)
    copies = [
        pltpu.make_async_copy(list_ref, list_smem, sem.at[0]),
        pltpu.make_async_copy(mult_ref, mult_smem, sem.at[1]),
    ]
    for copy in copies:
        copy.start()
    gather_moments(got_ref, rows, mom_ref, center_ref, take_ref, nblk, ndev, far_scale)
    widen_own(own_row, own_ref, nblk, range(6))
    far_into(own_ref, mom_ref, center_ref, acc_ref, nblk, mom_ref.shape[0])
    for copy in copies:
        copy.wait()
    near_into(
        lambda a, e, k: block_row(list_smem[a, e], k), coef_of, own_ref,
        lambda a: list_smem[a, LANES - 1], acc_ref, nblk,
    )
    sum_lanes(acc_ref, force_ref, nblk)
    pos, bur = [], []
    for k in range(3):
        here = slice(k * nblk, (k + 1) * nblk)
        vel = mob_ref[...] * force_ref[here, :]
        vel_ref[here, :] = vel
        for b in range(nblk):
            next_ref[k * nblk + b : k * nblk + b + 1, :] = own_row(k, b)
            next_ref[(3 + k) * nblk + b : (3 + k) * nblk + b + 1, :] = own_row(3 + k, b)
        moved = next_ref[here, :] + TIME_INCREMENT * vel
        next_ref[here, :] = moved
        pos.append(moved)
        bur.append(next_ref[(3 + k) * nblk : (4 + k) * nblk, :])
    last = moment_row(pos, bur, cells_ref, stack_ref)
    for r in range(3 * nblk):
        flat_ref[:, r * LANES : (r + 1) * LANES] = next_ref[r : r + 1, :]
    flat_ref[:, 3 * nblk * LANES :] = last
    spread(out_ref, flat_ref[...])


def third_kernel(
    n_slab, n_dom, far_scale,
    list_smem, mob_ref, pos_ref, vel_ref, old_ref, got_ref, coef_ref,
    moved_ref, velocity_ref,
    own_ref, acc_ref, force_ref, mom_ref, center_ref, take_ref,
):
    nblk = mob_ref.shape[0]
    ndev = n_slab * n_dom
    rows = got_ref.shape[0] // ndev
    old_rows = old_ref.shape[0] // ndev
    each = coef_ref.shape[0] // nblk
    me = lax.axis_index("slab") * n_dom + lax.axis_index("dom")

    def row_of(k, b):
        if k < 3:
            return got_ref[me * rows + k * nblk + b]
        return old_ref[me * old_rows + k * nblk + b]

    def block_row(a, e, k):
        g = list_smem[a, e]
        return got_ref[(g // nblk) * rows + g % nblk + k * nblk]

    def coef_of(a, e):
        return lambda t, rows: coef_ref[a * each + e, rows, :]

    gather_moments(got_ref, rows, mom_ref, center_ref, take_ref, nblk, ndev, far_scale)
    widen_own(row_of, own_ref, nblk, range(6))
    far_into(own_ref, mom_ref, center_ref, acc_ref, nblk, mom_ref.shape[0])
    near_into(block_row, coef_of, own_ref, lambda a: list_smem[a, LANES - 1], acc_ref, nblk)
    sum_lanes(acc_ref, force_ref, nblk)
    for k in range(3):
        here = slice(k * nblk, (k + 1) * nblk)
        force_ref[here, :] = 0.5 * (vel_ref[here, :] + mob_ref[...] * force_ref[here, :])
        for b in range(nblk):
            lanes = slice(b * LANES, (b + 1) * LANES)
            mean = force_ref[k * nblk + b : k * nblk + b + 1, :]
            velocity_ref[k : k + 1, lanes] = mean
            moved_ref[k : k + 1, lanes] = pos_ref[k : k + 1, lanes] + TIME_INCREMENT * mean


def body(positions, burgers, mobility, block_cells, pairs, pair_count):
    f32 = jnp.float32
    segs = positions.shape[1]
    nblk = block_cells.shape[0]
    n_slab, n_dom = lax.axis_size("slab"), lax.axis_size("dom")
    ndev = n_slab * n_dom
    far_scale = math.sqrt(16 * n_slab / (segs * ndev))
    rows, rows2 = 6 * nblk + 2, 3 * nblk + 1
    each = 9 * nblk + 2
    chunks = ndev * nblk // LANES
    high = -(-(3 * nblk) // SUB) * SUB
    scratch = [
        pltpu.VMEM((nblk, 6, LANES, LANES), f32),
        pltpu.VMEM((nblk, 3, LANES, LANES), f32),
        pltpu.VMEM((high, LANES), f32),
        pltpu.VMEM((chunks, LANES, LANES), f32),
        pltpu.VMEM((chunks, SUB, LANES), f32),
        pltpu.VMEM((LANES // nblk, LANES), f32),
    ]
    load, mob = pl.pallas_call(
        first_kernel,
        out_shape=(
            jax.ShapeDtypeStruct((ndev, 1, rows * LANES), f32),
            jax.ShapeDtypeStruct((nblk, LANES), f32),
        ),
        in_specs=[SMEM, SMEM, VMEM, VMEM, VMEM, VMEM],
        out_specs=(VMEM, VMEM),
        scratch_shapes=[
            pltpu.VMEM((LANES, LANES), f32),
            pltpu.VMEM((-(-rows // SUB) * SUB, LANES), f32),
            pltpu.VMEM((1, rows * LANES), f32),
        ],
        compiler_params=PARAMS,
        name="pack",
    )(block_cells, pair_count, positions, burgers, pairs, mobility.reshape(nblk, LANES))
    got = lax.all_to_all(load, ("slab", "dom"), 0, 0, tiled=True).reshape(ndev * rows, 1, LANES)
    load2, vel, lists, coef = pl.pallas_call(
        functools.partial(second_kernel, n_slab, n_dom, far_scale),
        out_shape=(
            jax.ShapeDtypeStruct((ndev, 1, rows2 * LANES), f32),
            jax.ShapeDtypeStruct((3 * nblk, LANES), f32),
            jax.ShapeDtypeStruct((SUB, LANES), jnp.int32),
            jax.ShapeDtypeStruct((nblk * each, LANES, LANES), f32),
        ),
        in_specs=[SMEM, VMEM, VMEM],
        out_specs=(VMEM, VMEM, VMEM, VMEM),
        scratch_shapes=[pltpu.VMEM((LANES, LANES), f32)]
        + scratch
        + [
            pltpu.VMEM((SUB, LANES), f32),
            pltpu.VMEM((SUB, LANES), f32),
            pltpu.VMEM((6 * nblk, LANES), f32),
            pltpu.VMEM((1, rows2 * LANES), f32),
            pltpu.SMEM((SUB, LANES), jnp.int32),
            pltpu.SMEM((SUB, LANES), f32),
            pltpu.SemaphoreType.DMA((2,)),
        ],
        compiler_params=PARAMS,
        name="step_one",
    )(block_cells, mob, got)
    got2 = lax.all_to_all(load2, ("slab", "dom"), 0, 0, tiled=True).reshape(ndev * rows2, 1, LANES)
    return pl.pallas_call(
        functools.partial(third_kernel, n_slab, n_dom, far_scale),
        out_shape=(jax.ShapeDtypeStruct((3, segs), f32),) * 2,
        in_specs=[SMEM, VMEM, VMEM, VMEM, VMEM, VMEM, VMEM],
        out_specs=(VMEM, VMEM),
        scratch_shapes=scratch,
        compiler_params=PARAMS,
        name="step_two",
    )(lists, mob, positions, vel, got, got2, coef)


def solution(mesh):
    placed = (
        P(None, ("slab", "dom")),
        P(None, ("slab", "dom")),
        P(("slab", "dom")),
        P(("slab", "dom")),
        P(("slab", "dom"), None),
        P(("slab", "dom")),
    )
    return jax.shard_map(
        body,
        mesh=mesh,
        in_specs=placed,
        out_specs=(P(None, ("slab", "dom")), P(None, ("slab", "dom"))),
        check_vma=False,
    )
```

```python
import functools
import math

import jax
import jax.numpy as jnp
from jax import lax
from jax.experimental import pallas as pl
from jax.experimental.pallas import tpu as pltpu
from jax.sharding import PartitionSpec as P


LANES = 128
SUB = 8
CORE_NEAR = 0.25
CORE_FAR = 9.0
TIME_INCREMENT = 0.25
EXACT = lax.Precision.HIGHEST
VMEM = pl.BlockSpec(memory_space=pltpu.VMEM)
SMEM = pl.BlockSpec(memory_space=pltpu.SMEM)
HBM = pl.BlockSpec(memory_space=pltpu.HBM)
PARAMS = pltpu.CompilerParams(vmem_limit_bytes=8 * 1024 * 1024)
SYM = ((0, 0), (0, 1), (0, 2), (1, 1), (1, 2), (2, 2))
MOMS = 3 + 9 + 18


def dot_lanes(a, b, precision=EXACT):
    return lax.dot_general(
        a, b, (((1,), (1,)), ((), ())), precision=precision, preferred_element_type=jnp.float32
    )


def center_of(cell):
    slab = jnp.floor(cell * 0.0625)
    rest = cell - 16.0 * slab
    row = jnp.floor(rest * 0.25)
    col = rest - 4.0 * row
    return (4.0 * slab + 2.0, 2.0 * row + 1.0, 2.0 * col + 1.0)


def column_of(values, like):
    index = lax.broadcasted_iota(jnp.int32, like, 0)
    out = jnp.full(like, values[-1], jnp.float32)
    for j, value in enumerate(values[:-1]):
        out = jnp.where(index == j, value, out)
    return out


def moment_row(pos, bur, cells_ref, stack_ref):
    nblk = pos[0].shape[0]
    cell = column_of([cells_ref[b].astype(jnp.float32) for b in range(nblk)], pos[0].shape)
    z = center_of(cell)
    d = [pos[k] - z[k] for k in range(3)]
    dd = [d[a] * d[e] for a, e in SYM]
    stack_ref[...] = jnp.zeros_like(stack_ref)
    m = 0
    for k in range(3):
        stack_ref[m * nblk : (m + 1) * nblk, :] = bur[k]
        m += 1
    for k in range(3):
        for a in range(3):
            stack_ref[m * nblk : (m + 1) * nblk, :] = bur[k] * d[a]
            m += 1
    for k in range(3):
        for j in range(6):
            stack_ref[m * nblk : (m + 1) * nblk, :] = bur[k] * dd[j]
            m += 1
    sums = dot_lanes(jnp.ones((SUB, LANES), jnp.float32), stack_ref[...])[0:1, :]
    lane = lax.broadcasted_iota(jnp.int32, (1, LANES), 1)
    for b in range(nblk):
        sums = jnp.where(lane == MOMS * nblk + b, cells_ref[b].astype(jnp.float32), sums)
    return sums


def spread(out_ref, value):
    count = out_ref.shape[0]

    def put(d, carry):
        out_ref[d] = value
        return carry

    lax.fori_loop(0, count, put, 0, unroll=math.gcd(count, 32))


def first_kernel(
    count_ref, cells_hbm, pos_hbm, bur_hbm, pairs_hbm, mob_hbm,
    out_ref, win_ref, mob_ref, cells_out_ref,
    pos_ref, bur_ref, pairs_ref, cells_ref, stack_ref, load_ref, flat_ref, ids_ref, sem,
):
    moves = (
        (cells_hbm, cells_ref), (pos_hbm, pos_ref), (bur_hbm, bur_ref),
        (pairs_hbm, pairs_ref), (mob_hbm, mob_ref), (cells_hbm, cells_out_ref),
    )
    copies = [pltpu.make_async_copy(src, dst, sem.at[j]) for j, (src, dst) in enumerate(moves)]
    for copy in copies:
        copy.start()
    for copy in copies:
        copy.wait()
    nblk = cells_ref.shape[0]
    slots = pairs_ref.shape[1]
    pos, bur = [], []
    for k in range(3):
        for b in range(nblk):
            lanes = slice(b * LANES, (b + 1) * LANES)
            load_ref[k * nblk + b : k * nblk + b + 1, :] = pos_ref[k : k + 1, lanes]
            load_ref[(3 + k) * nblk + b : (3 + k) * nblk + b + 1, :] = bur_ref[k : k + 1, lanes]
    for k in range(3):
        pos.append(load_ref[k * nblk : (k + 1) * nblk, :])
        bur.append(load_ref[(3 + k) * nblk : (4 + k) * nblk, :])
    ids_ref[0:1, 0:slots] = pairs_ref[0:1, :]
    ids_ref[0:1, slots : 2 * slots] = pairs_ref[1:2, :]
    slot = lax.broadcasted_iota(jnp.int32, (1, LANES), 1)
    slot = jnp.where(slot < slots, slot, slot - slots)
    listed = jnp.where(slot < count_ref[0], ids_ref[0:1, :], -1).astype(jnp.float32)
    for r in range(3 * nblk):
        lanes = slice(r * LANES, (r + 1) * LANES)
        flat_ref[:, lanes] = load_ref[r : r + 1, :]
        win_ref[0, :, lanes] = load_ref[3 * nblk + r : 3 * nblk + r + 1, :]
    win_ref[0, :, 3 * nblk * LANES :] = listed
    flat_ref[:, 3 * nblk * LANES :] = moment_row(pos, bur, cells_ref, stack_ref)
    spread(out_ref, flat_ref[...])


def far_into(own_ref, bur_ref, mom_ref, center_ref, acc_ref, nblk, chunks):
    def visit(c, a, first):
        for t in range(LANES // SUB):
            rows = slice(t * SUB, (t + 1) * SUB)

            def mom(m):
                return mom_ref[c, m * nblk : m * nblk + 1, :]

            b = [bur_ref[a, k, rows, :] for k in range(3)]
            r = [own_ref[a, k, rows, :] - center_ref[c, k : k + 1, :] for k in range(3)]
            sq = r[0] * r[0] + r[1] * r[1] + (r[2] * r[2] + CORE_FAR)
            inv = lax.rsqrt(sq)
            inv2 = inv * inv
            inv3 = inv2 * inv
            q0 = b[0] * mom(0) + b[1] * mom(1) + b[2] * mom(2)
            q1 = [b[0] * mom(3 + e) + b[1] * mom(6 + e) + b[2] * mom(9 + e) for e in range(3)]
            q2 = [b[0] * mom(12 + j) + b[1] * mom(18 + j) + b[2] * mom(24 + j) for j in range(6)]
            u = [
                q2[0] * r[0] + q2[1] * r[1] + q2[2] * r[2],
                q2[1] * r[0] + q2[3] * r[1] + q2[4] * r[2],
                q2[2] * r[0] + q2[4] * r[1] + q2[5] * r[2],
            ]
            q1r = q1[0] * r[0] + q1[1] * r[1] + q1[2] * r[2]
            rqr = u[0] * r[0] + u[1] * r[1] + u[2] * r[2]
            trace = q2[0] + q2[3] + q2[5]
            inner = (3.0 * q1r - 0.5 * trace) + (2.5 * rqr) * inv2
            scal = q0 + inner * inv2
            for k in range(3):
                f = (r[k] * scal - (q1[k] + inv2 * u[k])) * inv3
                acc_ref[a, k, rows, :] = f if first else acc_ref[a, k, rows, :] + f

    def start(a, carry):
        visit(0, a, True)
        return carry

    def more(n, carry):
        visit(1 + n // nblk, n % nblk, False)
        return carry

    lax.fori_loop(0, nblk, start, 0)
    if chunks > 1:
        lax.fori_loop(0, nblk * (chunks - 1), more, 0)


def near_into(row_pos, coef_of, own_ref, used_of, acc_ref, nblk):
    for a in range(nblk):

        def visit(n, carry):
            pair = (2 * n, 2 * n + 1)
            p = [[jnp.broadcast_to(row_pos(a, e, k), (SUB, LANES)) for k in range(3)] for e in pair]
            weigh = [coef_of(a, e) for e in pair]
            for t in range(LANES // SUB):
                rows = slice(t * SUB, (t + 1) * SUB)
                own = [own_ref[a, k, rows, :] for k in range(3)]
                f = []
                for j in range(2):
                    r = [own[k] - p[j][k] for k in range(3)]
                    sq = r[0] * r[0] + r[1] * r[1] + (r[2] * r[2] + CORE_NEAR)
                    u = lax.rsqrt(sq)
                    w = lax.rsqrt(sq + (CORE_FAR - CORE_NEAR))
                    wgt = weigh[j](t, rows) * (u * u * u - w * w * w)
                    f.append([wgt * r[k] for k in range(3)])
                for k in range(3):
                    acc_ref[a, k, rows, :] = acc_ref[a, k, rows, :] + (f[0][k] + f[1][k])
            return carry

        lax.fori_loop(0, (used_of(a) + 1) // 2, visit, 0)


def sum_lanes(acc_ref, force_ref, nblk):
    lane = lax.broadcasted_iota(jnp.int32, (SUB, LANES), 1)
    offset = lane - lax.broadcasted_iota(jnp.int32, (SUB, LANES), 0)
    for a in range(nblk):
        for k in range(3):
            out = jnp.zeros((SUB, LANES), jnp.float32)
            for t in range(LANES // SUB):
                total = jnp.sum(acc_ref[a, k, t * SUB : (t + 1) * SUB, :], axis=1, keepdims=True)
                out = jnp.where(offset == t * SUB, total, out)
            force_ref[k * nblk + a : k * nblk + a + 1, :] = jnp.sum(out, axis=0, keepdims=True)


def widen_own(row_of, own_ref, nblk):
    for a in range(nblk):
        for k in range(3):
            own_ref[a, k] = jnp.transpose(jnp.broadcast_to(row_of(k, a), (LANES, LANES)))


def window_ids(index, my_slab, my_dom, n_slab, n_dom, nblk):
    ids = jnp.full(index.shape, -2.0, jnp.float32)
    for k in range(9):
        s, e = my_slab + k % 3 - 1, my_dom + k // 3 - 1
        inside = (s >= 0) & (s < n_slab) & (e >= 0) & (e < n_dom)
        first = jnp.where(inside, (s * n_dom + e) * nblk - k * nblk, -100000)
        here = (index >= k * nblk) & (index < (k + 1) * nblk)
        ids = jnp.where(here, (index + first).astype(jnp.float32), ids)
    return ids


def build_lists(win_ref, rows, nblk, my_slab, my_dom, n_slab, n_dom, count_ref, list_ref, mult_ref):
    high = -(-9 * nblk // SUB) * SUB
    place = (my_slab, my_dom, n_slab, n_dom, nblk)
    gid = window_ids(lax.broadcasted_iota(jnp.int32, (high, LANES), 0), *place)
    own = (my_slab * n_dom + my_dom) * nblk
    sub = lax.broadcasted_iota(jnp.int32, (SUB, LANES), 0)
    lane = lax.broadcasted_iota(jnp.int32, (SUB, LANES), 1)
    mine = jnp.where(sub < nblk, sub + own, -3).astype(jnp.float32)
    total = jnp.zeros((SUB, high), jnp.float32)
    for k in range(9):
        s, e = my_slab + k % 3 - 1, my_dom + k // 3 - 1
        inside = (s >= 0) & (s < n_slab) & (e >= 0) & (e < n_dom)
        row = jnp.where(inside, win_ref[k * rows + rows - 1], -1.0)
        other = pltpu.roll(row, LANES // 2, 1)
        left = (mine == row).astype(jnp.float32)
        right = (gid == other).astype(jnp.float32)
        total = total + dot_lanes(left, right, None)
    count_ref[...] = jnp.zeros_like(count_ref)
    count_ref[:, 0:high] = total
    count = count_ref[...]
    met = jnp.where(count > 0.5, 1.0, 0.0)
    before = lax.broadcasted_iota(jnp.int32, (LANES, LANES), 1) < lax.broadcasted_iota(
        jnp.int32, (LANES, LANES), 0
    )
    rank = dot_lanes(met, before.astype(jnp.float32), None)
    used = jnp.sum(met, axis=1, keepdims=True).astype(jnp.int32)
    list_ref[...] = jnp.where(lane == LANES - 1, used, 0)
    mult_ref[...] = jnp.zeros_like(mult_ref)
    line = window_ids(lane, *place)
    here = lane.astype(jnp.float32)
    spot = lax.broadcasted_iota(jnp.int32, (high, LANES), 0).astype(jnp.float32)
    for a in range(nblk):
        pick = (rank[a : a + 1, :] == spot) & (met[a : a + 1, :] > 0.5)
        what = jnp.where(sub == 0, line, jnp.where(sub == 1, count[a : a + 1, :], here))
        out = dot_lanes(what, pick.astype(jnp.float32))
        list_ref[a : a + 1, 0:high] = (out[0:1, :] + 0.5).astype(jnp.int32)
        mult_ref[a : a + 1, 0:high] = out[1:2, :]
        list_ref[nblk + a : nblk + a + 1, 0:high] = (out[2:3, :] + 0.5).astype(jnp.int32)


def gather_moments(got_ref, rows, mom_ref, center_ref, take_ref, nblk, ndev, far_scale):
    width = LANES // nblk
    for c in range(ndev // width):

        def take(d, carry):
            take_ref[pl.ds(d, 1), :] = got_ref[(c * width + d) * rows + rows - 1]
            return carry

        lax.fori_loop(0, width, take, 0, unroll=True)
        block = take_ref[...]
        turned = [block] + [pltpu.roll(block, LANES - b, 1) for b in range(1, nblk)]
        flat = jnp.transpose(jnp.concatenate(turned, axis=0))
        z = center_of(flat[MOMS * nblk : MOMS * nblk + 1, :])
        for k in range(3):
            center_ref[c, k : k + 1, :] = z[k]
        row = lax.broadcasted_iota(jnp.int32, (LANES, LANES), 0)
        mom_ref[c] = flat * jnp.where(row < 12 * nblk, far_scale, 3.0 * far_scale)


def second_kernel(
    n_slab, n_dom, far_scale,
    cells_ref, mob_ref, got_ref, low_ref, mid_ref, high_ref,
    out_ref, vel_ref, list_ref, coef_ref, wide_ref, moved_ref,
    stack_ref, own_ref, acc_ref, force_ref, mom_ref, center_ref, take_ref,
    win_ref, count_ref, mult_ref, next_ref, flat_ref, list_smem, mult_smem, sem,
):
    nblk = cells_ref.shape[0]
    ndev = n_slab * n_dom
    rows = got_ref.shape[0] // ndev
    each = coef_ref.shape[0] // nblk
    my_slab, my_dom = lax.axis_index("slab"), lax.axis_index("dom")
    me = my_slab * n_dom + my_dom
    third = low_ref.shape[0]
    places = third // 3
    for j, ref in enumerate((low_ref, mid_ref, high_ref)):
        win_ref[j * third : (j + 1) * third] = ref[...]

    def own_row(k, b):
        return got_ref[me * rows + k * nblk + b]

    def own_bur(k, b):
        return win_ref[4 * places + k * nblk + b]

    def block_row(a, e, k):
        g = list_smem[a, e]
        return got_ref[(g // nblk) * rows + g % nblk + k * nblk]

    def coef_of(a, e):
        w, mult = list_smem[nblk + a, e], mult_smem[a, e]
        first = (w // nblk) * places + w % nblk
        c = [jnp.broadcast_to(win_ref[first + k * nblk] * mult, (SUB, LANES)) for k in range(3)]

        def tile(t, rows):
            value = wide_ref[a, 0, rows, :] * c[0] + wide_ref[a, 1, rows, :] * c[1] + wide_ref[a, 2, rows, :] * c[2]
            coef_ref[a * each + e, rows, :] = value
            return value

        return tile

    build_lists(win_ref, places, nblk, my_slab, my_dom, n_slab, n_dom, count_ref, list_ref, mult_ref)
    copies = [
        pltpu.make_async_copy(list_ref, list_smem, sem.at[0]),
        pltpu.make_async_copy(mult_ref, mult_smem, sem.at[1]),
    ]
    for copy in copies:
        copy.start()
    gather_moments(got_ref, rows, mom_ref, center_ref, take_ref, nblk, ndev, far_scale)
    widen_own(own_row, own_ref, nblk)
    widen_own(own_bur, wide_ref, nblk)
    far_into(own_ref, wide_ref, mom_ref, center_ref, acc_ref, nblk, mom_ref.shape[0])
    for copy in copies:
        copy.wait()
    near_into(block_row, coef_of, own_ref, lambda a: list_smem[a, LANES - 1], acc_ref, nblk)
    sum_lanes(acc_ref, force_ref, nblk)
    pos, bur = [], []
    for k in range(3):
        here = slice(k * nblk, (k + 1) * nblk)
        vel = mob_ref[...] * force_ref[here, :]
        vel_ref[here, :] = vel
        for b in range(nblk):
            next_ref[k * nblk + b : k * nblk + b + 1, :] = own_row(k, b)
            next_ref[(3 + k) * nblk + b : (3 + k) * nblk + b + 1, :] = own_bur(k, b)
        moved = next_ref[here, :] + TIME_INCREMENT * vel
        moved_ref[here, :] = moved
        pos.append(moved)
        bur.append(next_ref[(3 + k) * nblk : (4 + k) * nblk, :])
    last = moment_row(pos, bur, cells_ref, stack_ref)
    for r in range(3 * nblk):
        flat_ref[:, r * LANES : (r + 1) * LANES] = moved_ref[r : r + 1, :]
    flat_ref[:, 3 * nblk * LANES :] = last
    spread(out_ref, flat_ref[...])


def third_kernel(
    n_slab, n_dom, far_scale,
    list_smem, mob_ref, vel_ref, old_ref, got_ref, coef_ref, wide_ref, next_ref,
    moved_ref, velocity_ref,
    own_ref, acc_ref, force_ref, mom_ref, center_ref, take_ref,
):
    nblk = mob_ref.shape[0]
    ndev = n_slab * n_dom
    rows = got_ref.shape[0] // ndev
    each = coef_ref.shape[0] // nblk
    me = lax.axis_index("slab") * n_dom + lax.axis_index("dom")

    def block_row(a, e, k):
        g = list_smem[a, e]
        return got_ref[(g // nblk) * rows + g % nblk + k * nblk]

    def coef_of(a, e):
        return lambda t, rows: coef_ref[a * each + e, rows, :]

    widen_own(lambda k, b: next_ref[k * nblk + b : k * nblk + b + 1, :], own_ref, nblk)
    gather_moments(got_ref, rows, mom_ref, center_ref, take_ref, nblk, ndev, far_scale)
    far_into(own_ref, wide_ref, mom_ref, center_ref, acc_ref, nblk, mom_ref.shape[0])
    near_into(block_row, coef_of, own_ref, lambda a: list_smem[a, LANES - 1], acc_ref, nblk)
    sum_lanes(acc_ref, force_ref, nblk)
    for k in range(3):
        here = slice(k * nblk, (k + 1) * nblk)
        force_ref[here, :] = 0.5 * (vel_ref[here, :] + mob_ref[...] * force_ref[here, :])
        for b in range(nblk):
            lanes = slice(b * LANES, (b + 1) * LANES)
            mean = force_ref[k * nblk + b : k * nblk + b + 1, :]
            velocity_ref[k : k + 1, lanes] = mean
            moved_ref[k : k + 1, lanes] = old_ref[me * rows + k * nblk + b] + TIME_INCREMENT * mean


def neighbours(x, axis):
    count = lax.axis_size(axis)
    below = lax.ppermute(x, axis, [(i, (i + 1) % count) for i in range(count)])
    above = lax.ppermute(x, axis, [((i + 1) % count, i) for i in range(count)])
    return below, above


def body(positions, burgers, mobility, block_cells, pairs, pair_count):
    f32 = jnp.float32
    segs = positions.shape[1]
    nblk = block_cells.shape[0]
    slots = pairs.shape[0]
    n_slab, n_dom = lax.axis_size("slab"), lax.axis_size("dom")
    ndev = n_slab * n_dom
    far_scale = math.sqrt(16 * n_slab / (segs * ndev))
    rows = 3 * nblk + 1
    each = 9 * nblk + 2
    chunks = ndev * nblk // LANES
    high = -(-(3 * nblk) // SUB) * SUB
    wide = jax.ShapeDtypeStruct((nblk, 3, LANES, LANES), f32)
    payload = jax.ShapeDtypeStruct((ndev, 1, rows * LANES), f32)
    scratch = [
        pltpu.VMEM((nblk, 3, LANES, LANES), f32),
        pltpu.VMEM((high, LANES), f32),
        pltpu.VMEM((chunks, LANES, LANES), f32),
        pltpu.VMEM((chunks, SUB, LANES), f32),
        pltpu.VMEM((LANES // nblk, LANES), f32),
    ]
    load, window, mob, cells = pl.pallas_call(
        first_kernel,
        out_shape=(
            payload,
            jax.ShapeDtypeStruct((1, 1, rows * LANES), f32),
            jax.ShapeDtypeStruct((nblk, LANES), f32),
            jax.ShapeDtypeStruct((nblk,), jnp.int32),
        ),
        in_specs=[SMEM] + [HBM] * 5,
        out_specs=(VMEM,) * 4,
        scratch_shapes=[
            pltpu.VMEM((3, segs), f32),
            pltpu.VMEM((3, segs), f32),
            pltpu.VMEM((2, slots), jnp.int32),
            pltpu.SMEM((nblk,), jnp.int32),
            pltpu.VMEM((LANES, LANES), f32),
            pltpu.VMEM((-(-6 * nblk // SUB) * SUB, LANES), f32),
            pltpu.VMEM((1, rows * LANES), f32),
            pltpu.VMEM((SUB, LANES), jnp.int32),
            pltpu.SemaphoreType.DMA((6,)),
        ],
        compiler_params=PARAMS,
        name="pack",
    )(
        pair_count,
        *(
            pltpu.with_memory_space_constraint(x, pltpu.HBM)
            for x in (block_cells, positions, burgers, pairs.T, mobility.reshape(nblk, LANES))
        ),
    )
    got = lax.all_to_all(load, ("slab", "dom"), 0, 0, tiled=True).reshape(ndev * rows, 1, LANES)
    below, above = neighbours(window, "slab")
    column = jnp.concatenate([below, window, above], axis=0)
    left, right = neighbours(column, "dom")
    left, column, right = (x.reshape(3 * rows, 1, LANES) for x in (left, column, right))
    load2, vel, lists, coef, bur_wide, moved = pl.pallas_call(
        functools.partial(second_kernel, n_slab, n_dom, far_scale),
        out_shape=(
            payload,
            jax.ShapeDtypeStruct((3 * nblk, LANES), f32),
            jax.ShapeDtypeStruct((SUB, LANES), jnp.int32),
            jax.ShapeDtypeStruct((nblk * each, LANES, LANES), f32),
            wide,
            jax.ShapeDtypeStruct((3 * nblk, LANES), f32),
        ),
        in_specs=[SMEM] + [VMEM] * 5,
        out_specs=(VMEM,) * 6,
        scratch_shapes=[pltpu.VMEM((LANES, LANES), f32), pltpu.VMEM((nblk, 3, LANES, LANES), f32)]
        + scratch
        + [
            pltpu.VMEM((9 * rows, 1, LANES), f32),
            pltpu.VMEM((SUB, LANES), f32),
            pltpu.VMEM((SUB, LANES), f32),
            pltpu.VMEM((6 * nblk, LANES), f32),
            pltpu.VMEM((1, rows * LANES), f32),
            pltpu.SMEM((SUB, LANES), jnp.int32),
            pltpu.SMEM((SUB, LANES), f32),
            pltpu.SemaphoreType.DMA((2,)),
        ],
        compiler_params=PARAMS,
        name="step_one",
    )(cells, mob, got, left, column, right)
    got2 = lax.all_to_all(load2, ("slab", "dom"), 0, 0, tiled=True).reshape(ndev * rows, 1, LANES)
    return pl.pallas_call(
        functools.partial(third_kernel, n_slab, n_dom, far_scale),
        out_shape=(jax.ShapeDtypeStruct((3, segs), f32),) * 2,
        in_specs=[SMEM] + [VMEM] * 7,
        out_specs=(VMEM, VMEM),
        scratch_shapes=[pltpu.VMEM((nblk, 3, LANES, LANES), f32)] + scratch,
        compiler_params=PARAMS,
        name="step_two",
    )(lists, mob, vel, got, got2, coef, bur_wide, moved)


def solution(mesh):
    placed = (
        P(None, ("slab", "dom")),
        P(None, ("slab", "dom")),
        P(("slab", "dom")),
        P(("slab", "dom")),
        P(("slab", "dom"), None),
        P(("slab", "dom")),
    )
    return jax.shard_map(
        body,
        mesh=mesh,
        in_specs=placed,
        out_specs=(P(None, ("slab", "dom")), P(None, ("slab", "dom"))),
        check_vma=False,
    )
```

```python
import functools
import math

import jax
import jax.numpy as jnp
from jax import lax
from jax.experimental import pallas as pl
from jax.experimental.pallas import tpu as pltpu
from jax.sharding import PartitionSpec as P


LANES = 128
SUB = 8
CORE_NEAR = 0.25
CORE_FAR = 9.0
TIME_INCREMENT = 0.25
EXACT = lax.Precision.HIGHEST
VMEM = pl.BlockSpec(memory_space=pltpu.VMEM)
SMEM = pl.BlockSpec(memory_space=pltpu.SMEM)
HBM = pl.BlockSpec(memory_space=pltpu.HBM)
PARAMS = pltpu.CompilerParams(vmem_limit_bytes=8 * 1024 * 1024)
SYM = ((0, 0), (0, 1), (0, 2), (1, 1), (1, 2), (2, 2))
MOMS = 3 + 9 + 18


def dot_lanes(a, b, precision=EXACT):
    return lax.dot_general(
        a, b, (((1,), (1,)), ((), ())), precision=precision, preferred_element_type=jnp.float32
    )


def center_of(cell):
    slab = jnp.floor(cell * 0.0625)
    rest = cell - 16.0 * slab
    row = jnp.floor(rest * 0.25)
    col = rest - 4.0 * row
    return (4.0 * slab + 2.0, 2.0 * row + 1.0, 2.0 * col + 1.0)


def column_of(values, like):
    index = lax.broadcasted_iota(jnp.int32, like, 0)
    out = jnp.full(like, values[-1], jnp.float32)
    for j, value in enumerate(values[:-1]):
        out = jnp.where(index == j, value, out)
    return out


def moment_row(pos, bur, cells_ref, stack_ref):
    nblk = pos[0].shape[0]
    cell = column_of([cells_ref[b].astype(jnp.float32) for b in range(nblk)], pos[0].shape)
    z = center_of(cell)
    d = [pos[k] - z[k] for k in range(3)]
    dd = [d[a] * d[e] for a, e in SYM]
    stack_ref[...] = jnp.zeros_like(stack_ref)
    m = 0
    for k in range(3):
        stack_ref[m * nblk : (m + 1) * nblk, :] = bur[k]
        m += 1
    for k in range(3):
        for a in range(3):
            stack_ref[m * nblk : (m + 1) * nblk, :] = bur[k] * d[a]
            m += 1
    for k in range(3):
        for j in range(6):
            stack_ref[m * nblk : (m + 1) * nblk, :] = bur[k] * dd[j]
            m += 1
    sums = dot_lanes(jnp.ones((SUB, LANES), jnp.float32), stack_ref[...])[0:1, :]
    lane = lax.broadcasted_iota(jnp.int32, (1, LANES), 1)
    for b in range(nblk):
        sums = jnp.where(lane == MOMS * nblk + b, cells_ref[b].astype(jnp.float32), sums)
    return sums


def spread(out_ref, value):
    count = out_ref.shape[0]

    def put(d, carry):
        out_ref[d] = value
        return carry

    lax.fori_loop(0, count, put, 0, unroll=math.gcd(count, 32))


def first_kernel(
    count_ref, cells_hbm, pos_hbm, bur_hbm, pairs_hbm, mob_hbm,
    out_ref, win_ref, mob_ref, cells_out_ref,
    pos_ref, bur_ref, pairs_ref, cells_ref, stack_ref, load_ref, ids_ref, sem,
):
    moves = (
        (cells_hbm, cells_ref), (pos_hbm, pos_ref), (bur_hbm, bur_ref),
        (pairs_hbm, pairs_ref), (mob_hbm, mob_ref), (cells_hbm, cells_out_ref),
    )
    copies = [pltpu.make_async_copy(src, dst, sem.at[j]) for j, (src, dst) in enumerate(moves)]
    for copy in copies:
        copy.start()
    for copy in copies:
        copy.wait()
    nblk = cells_ref.shape[0]
    slots = pairs_ref.shape[1]
    pos, bur = [], []
    for k in range(3):
        for b in range(nblk):
            lanes = slice(b * LANES, (b + 1) * LANES)
            load_ref[k * nblk + b : k * nblk + b + 1, :] = pos_ref[k : k + 1, lanes]
            load_ref[(3 + k) * nblk + b : (3 + k) * nblk + b + 1, :] = bur_ref[k : k + 1, lanes]
    for k in range(3):
        pos.append(load_ref[k * nblk : (k + 1) * nblk, :])
        bur.append(load_ref[(3 + k) * nblk : (4 + k) * nblk, :])
    ids_ref[0:1, 0:slots] = pairs_ref[0:1, :]
    ids_ref[0:1, slots : 2 * slots] = pairs_ref[1:2, :]
    slot = lax.broadcasted_iota(jnp.int32, (1, LANES), 1)
    slot = jnp.where(slot < slots, slot, slot - slots)
    listed = jnp.where(slot < count_ref[0], ids_ref[0:1, :], -1).astype(jnp.float32)
    for r in range(6 * nblk):
        win_ref[0, :, r * LANES : (r + 1) * LANES] = load_ref[r : r + 1, :]
    win_ref[0, :, 6 * nblk * LANES :] = listed
    spread(out_ref, moment_row(pos, bur, cells_ref, stack_ref))


def far_into(own_ref, bur_ref, mom_ref, center_ref, acc_ref, nblk, chunks):
    def visit(c, a, first):
        for t in range(LANES // SUB):
            rows = slice(t * SUB, (t + 1) * SUB)

            def mom(m):
                return mom_ref[c, m * nblk : m * nblk + 1, :]

            b = [bur_ref[a, k, rows, :] for k in range(3)]
            r = [own_ref[a, k, rows, :] - center_ref[c, k : k + 1, :] for k in range(3)]
            sq = r[0] * r[0] + r[1] * r[1] + (r[2] * r[2] + CORE_FAR)
            inv = lax.rsqrt(sq)
            inv2 = inv * inv
            inv3 = inv2 * inv
            q0 = b[0] * mom(0) + b[1] * mom(1) + b[2] * mom(2)
            q1 = [b[0] * mom(3 + e) + b[1] * mom(6 + e) + b[2] * mom(9 + e) for e in range(3)]
            q2 = [b[0] * mom(12 + j) + b[1] * mom(18 + j) + b[2] * mom(24 + j) for j in range(6)]
            u = [
                q2[0] * r[0] + q2[1] * r[1] + q2[2] * r[2],
                q2[1] * r[0] + q2[3] * r[1] + q2[4] * r[2],
                q2[2] * r[0] + q2[4] * r[1] + q2[5] * r[2],
            ]
            q1r = q1[0] * r[0] + q1[1] * r[1] + q1[2] * r[2]
            rqr = u[0] * r[0] + u[1] * r[1] + u[2] * r[2]
            trace = q2[0] + q2[3] + q2[5]
            inner = (3.0 * q1r - 0.5 * trace) + (2.5 * rqr) * inv2
            scal = q0 + inner * inv2
            for k in range(3):
                f = (r[k] * scal - (q1[k] + inv2 * u[k])) * inv3
                acc_ref[a, k, rows, :] = f if first else acc_ref[a, k, rows, :] + f

    def start(a, carry):
        visit(0, a, True)
        return carry

    def more(n, carry):
        visit(1 + n // nblk, n % nblk, False)
        return carry

    lax.fori_loop(0, nblk, start, 0)
    if chunks > 1:
        lax.fori_loop(0, nblk * (chunks - 1), more, 0)


def near_into(row_pos, coef_of, own_ref, used_of, acc_ref, nblk):
    for a in range(nblk):

        def visit(n, carry):
            pair = (2 * n, 2 * n + 1)
            p = [[jnp.broadcast_to(row_pos(a, e, k), (SUB, LANES)) for k in range(3)] for e in pair]
            weigh = [coef_of(a, e) for e in pair]
            for t in range(LANES // SUB):
                rows = slice(t * SUB, (t + 1) * SUB)
                own = [own_ref[a, k, rows, :] for k in range(3)]
                f = []
                for j in range(2):
                    r = [own[k] - p[j][k] for k in range(3)]
                    sq = r[0] * r[0] + r[1] * r[1] + (r[2] * r[2] + CORE_NEAR)
                    u = lax.rsqrt(sq)
                    w = lax.rsqrt(sq + (CORE_FAR - CORE_NEAR))
                    wgt = weigh[j](t, rows) * (u * u * u - w * w * w)
                    f.append([wgt * r[k] for k in range(3)])
                for k in range(3):
                    acc_ref[a, k, rows, :] = acc_ref[a, k, rows, :] + (f[0][k] + f[1][k])
            return carry

        lax.fori_loop(0, (used_of(a) + 1) // 2, visit, 0)


def sum_lanes(acc_ref, force_ref, nblk):
    lane = lax.broadcasted_iota(jnp.int32, (SUB, LANES), 1)
    offset = lane - lax.broadcasted_iota(jnp.int32, (SUB, LANES), 0)
    for a in range(nblk):
        for k in range(3):
            out = jnp.zeros((SUB, LANES), jnp.float32)
            for t in range(LANES // SUB):
                total = jnp.sum(acc_ref[a, k, t * SUB : (t + 1) * SUB, :], axis=1, keepdims=True)
                out = jnp.where(offset == t * SUB, total, out)
            force_ref[k * nblk + a : k * nblk + a + 1, :] = jnp.sum(out, axis=0, keepdims=True)


def widen_own(row_of, own_ref, nblk):
    for a in range(nblk):
        for k in range(3):
            own_ref[a, k] = jnp.transpose(jnp.broadcast_to(row_of(k, a), (LANES, LANES)))


def window_ids(index, my_slab, my_dom, n_slab, n_dom, nblk):
    ids = jnp.full(index.shape, -2.0, jnp.float32)
    for k in range(9):
        s, e = my_slab + k % 3 - 1, my_dom + k // 3 - 1
        inside = (s >= 0) & (s < n_slab) & (e >= 0) & (e < n_dom)
        first = jnp.where(inside, (s * n_dom + e) * nblk - k * nblk, -100000)
        here = (index >= k * nblk) & (index < (k + 1) * nblk)
        ids = jnp.where(here, (index + first).astype(jnp.float32), ids)
    return ids


def build_lists(win_ref, rows, nblk, my_slab, my_dom, n_slab, n_dom, count_ref, list_ref, mult_ref):
    high = -(-9 * nblk // SUB) * SUB
    place = (my_slab, my_dom, n_slab, n_dom, nblk)
    gid = window_ids(lax.broadcasted_iota(jnp.int32, (high, LANES), 0), *place)
    own = (my_slab * n_dom + my_dom) * nblk
    sub = lax.broadcasted_iota(jnp.int32, (SUB, LANES), 0)
    lane = lax.broadcasted_iota(jnp.int32, (SUB, LANES), 1)
    mine = jnp.where(sub < nblk, sub + own, -3).astype(jnp.float32)
    total = jnp.zeros((SUB, high), jnp.float32)
    for k in range(9):
        s, e = my_slab + k % 3 - 1, my_dom + k // 3 - 1
        inside = (s >= 0) & (s < n_slab) & (e >= 0) & (e < n_dom)
        row = jnp.where(inside, win_ref[k * rows + rows - 1], -1.0)
        other = pltpu.roll(row, LANES // 2, 1)
        left = (mine == row).astype(jnp.float32)
        right = (gid == other).astype(jnp.float32)
        total = total + dot_lanes(left, right, None)
    count_ref[...] = jnp.zeros_like(count_ref)
    count_ref[:, 0:high] = total
    count = count_ref[...]
    met = jnp.where(count > 0.5, 1.0, 0.0)
    before = lax.broadcasted_iota(jnp.int32, (LANES, LANES), 1) < lax.broadcasted_iota(
        jnp.int32, (LANES, LANES), 0
    )
    rank = dot_lanes(met, before.astype(jnp.float32), None)
    used = jnp.sum(met, axis=1, keepdims=True).astype(jnp.int32)
    list_ref[...] = jnp.where(lane == LANES - 1, used, 0)
    mult_ref[...] = jnp.zeros_like(mult_ref)
    line = window_ids(lane, *place)
    here = lane.astype(jnp.float32)
    spot = lax.broadcasted_iota(jnp.int32, (high, LANES), 0).astype(jnp.float32)
    for a in range(nblk):
        pick = (rank[a : a + 1, :] == spot) & (met[a : a + 1, :] > 0.5)
        what = jnp.where(sub == 0, line, jnp.where(sub == 1, count[a : a + 1, :], here))
        out = dot_lanes(what, pick.astype(jnp.float32))
        list_ref[a : a + 1, 0:high] = (out[0:1, :] + 0.5).astype(jnp.int32)
        mult_ref[a : a + 1, 0:high] = out[1:2, :]
        list_ref[nblk + a : nblk + a + 1, 0:high] = (out[2:3, :] + 0.5).astype(jnp.int32)


def gather_moments(got_ref, rows, mom_ref, center_ref, take_ref, nblk, ndev, far_scale):
    width = LANES // nblk
    for c in range(ndev // width):

        def take(d, carry):
            take_ref[pl.ds(d, 1), :] = got_ref[(c * width + d) * rows + rows - 1]
            return carry

        lax.fori_loop(0, width, take, 0, unroll=True)
        block = take_ref[...]
        turned = [block] + [pltpu.roll(block, LANES - b, 1) for b in range(1, nblk)]
        flat = jnp.transpose(jnp.concatenate(turned, axis=0))
        z = center_of(flat[MOMS * nblk : MOMS * nblk + 1, :])
        for k in range(3):
            center_ref[c, k : k + 1, :] = z[k]
        row = lax.broadcasted_iota(jnp.int32, (LANES, LANES), 0)
        mom_ref[c] = flat * jnp.where(row < 12 * nblk, far_scale, 3.0 * far_scale)


def second_kernel(
    n_slab, n_dom, far_scale,
    cells_ref, mob_ref, got_ref, low_ref, mid_ref, high_ref,
    out_ref, vel_ref, list_ref, coef_ref, wide_ref, moved_ref, old_ref,
    stack_ref, own_ref, acc_ref, force_ref, mom_ref, center_ref, take_ref,
    win_ref, count_ref, mult_ref, next_ref, flat_ref, list_smem, mult_smem, sem,
):
    nblk = cells_ref.shape[0]
    ndev = n_slab * n_dom
    rows = got_ref.shape[0] // ndev
    each = coef_ref.shape[0] // nblk
    my_slab, my_dom = lax.axis_index("slab"), lax.axis_index("dom")
    third = low_ref.shape[0]
    places = third // 3
    for j, ref in enumerate((low_ref, mid_ref, high_ref)):
        win_ref[j * third : (j + 1) * third] = ref[...]

    def own_row(k, b):
        return win_ref[4 * places + k * nblk + b]

    def own_bur(k, b):
        return own_row(3 + k, b)

    def block_row(a, e, k):
        w = list_smem[nblk + a, e]
        return win_ref[(w // nblk) * places + w % nblk + k * nblk]

    def coef_of(a, e):
        mult = mult_smem[a, e]
        c = [jnp.broadcast_to(block_row(a, e, 3 + k) * mult, (SUB, LANES)) for k in range(3)]

        def tile(t, rows):
            value = wide_ref[a, 0, rows, :] * c[0] + wide_ref[a, 1, rows, :] * c[1] + wide_ref[a, 2, rows, :] * c[2]
            coef_ref[a * each + e, rows, :] = value
            return value

        return tile

    build_lists(win_ref, places, nblk, my_slab, my_dom, n_slab, n_dom, count_ref, list_ref, mult_ref)
    copies = [
        pltpu.make_async_copy(list_ref, list_smem, sem.at[0]),
        pltpu.make_async_copy(mult_ref, mult_smem, sem.at[1]),
    ]
    for copy in copies:
        copy.start()
    gather_moments(got_ref, rows, mom_ref, center_ref, take_ref, nblk, ndev, far_scale)
    widen_own(own_row, own_ref, nblk)
    widen_own(own_bur, wide_ref, nblk)
    far_into(own_ref, wide_ref, mom_ref, center_ref, acc_ref, nblk, mom_ref.shape[0])
    for copy in copies:
        copy.wait()
    near_into(block_row, coef_of, own_ref, lambda a: list_smem[a, LANES - 1], acc_ref, nblk)
    sum_lanes(acc_ref, force_ref, nblk)
    pos, bur = [], []
    for k in range(3):
        here = slice(k * nblk, (k + 1) * nblk)
        vel = mob_ref[...] * force_ref[here, :]
        vel_ref[here, :] = vel
        for b in range(nblk):
            next_ref[k * nblk + b : k * nblk + b + 1, :] = own_row(k, b)
            next_ref[(3 + k) * nblk + b : (3 + k) * nblk + b + 1, :] = own_bur(k, b)
        old_ref[here, :] = next_ref[here, :]
        moved = next_ref[here, :] + TIME_INCREMENT * vel
        moved_ref[here, :] = moved
        pos.append(moved)
        bur.append(next_ref[(3 + k) * nblk : (4 + k) * nblk, :])
    last = moment_row(pos, bur, cells_ref, stack_ref)
    for r in range(3 * nblk):
        flat_ref[:, r * LANES : (r + 1) * LANES] = moved_ref[r : r + 1, :]
    flat_ref[:, 3 * nblk * LANES :] = last
    spread(out_ref, flat_ref[...])


def third_kernel(
    n_slab, n_dom, far_scale,
    list_smem, mob_ref, vel_ref, old_ref, got_ref, coef_ref, wide_ref, next_ref,
    moved_ref, velocity_ref,
    own_ref, acc_ref, force_ref, mom_ref, center_ref, take_ref,
):
    nblk = mob_ref.shape[0]
    ndev = n_slab * n_dom
    rows = got_ref.shape[0] // ndev
    each = coef_ref.shape[0] // nblk

    def block_row(a, e, k):
        g = list_smem[a, e]
        return got_ref[(g // nblk) * rows + g % nblk + k * nblk]

    def coef_of(a, e):
        return lambda t, rows: coef_ref[a * each + e, rows, :]

    widen_own(lambda k, b: next_ref[k * nblk + b : k * nblk + b + 1, :], own_ref, nblk)
    gather_moments(got_ref, rows, mom_ref, center_ref, take_ref, nblk, ndev, far_scale)
    far_into(own_ref, wide_ref, mom_ref, center_ref, acc_ref, nblk, mom_ref.shape[0])
    near_into(block_row, coef_of, own_ref, lambda a: list_smem[a, LANES - 1], acc_ref, nblk)
    sum_lanes(acc_ref, force_ref, nblk)
    for k in range(3):
        here = slice(k * nblk, (k + 1) * nblk)
        force_ref[here, :] = 0.5 * (vel_ref[here, :] + mob_ref[...] * force_ref[here, :])
        for b in range(nblk):
            lanes = slice(b * LANES, (b + 1) * LANES)
            mean = force_ref[k * nblk + b : k * nblk + b + 1, :]
            velocity_ref[k : k + 1, lanes] = mean
            moved_ref[k : k + 1, lanes] = old_ref[k * nblk + b : k * nblk + b + 1, :] + TIME_INCREMENT * mean


def neighbours(x, axis):
    count = lax.axis_size(axis)
    below = lax.ppermute(x, axis, [(i, (i + 1) % count) for i in range(count)])
    above = lax.ppermute(x, axis, [((i + 1) % count, i) for i in range(count)])
    return below, above


def body(positions, burgers, mobility, block_cells, pairs, pair_count):
    f32 = jnp.float32
    segs = positions.shape[1]
    nblk = block_cells.shape[0]
    slots = pairs.shape[0]
    n_slab, n_dom = lax.axis_size("slab"), lax.axis_size("dom")
    ndev = n_slab * n_dom
    far_scale = math.sqrt(16 * n_slab / (segs * ndev))
    rows, places = 3 * nblk + 1, 6 * nblk + 1
    each = 9 * nblk + 2
    chunks = ndev * nblk // LANES
    high = -(-(3 * nblk) // SUB) * SUB
    wide = jax.ShapeDtypeStruct((nblk, 3, LANES, LANES), f32)
    payload = jax.ShapeDtypeStruct((ndev, 1, rows * LANES), f32)
    scratch = [
        pltpu.VMEM((nblk, 3, LANES, LANES), f32),
        pltpu.VMEM((high, LANES), f32),
        pltpu.VMEM((chunks, LANES, LANES), f32),
        pltpu.VMEM((chunks, SUB, LANES), f32),
        pltpu.VMEM((LANES // nblk, LANES), f32),
    ]
    load, window, mob, cells = pl.pallas_call(
        first_kernel,
        out_shape=(
            jax.ShapeDtypeStruct((ndev, 1, LANES), f32),
            jax.ShapeDtypeStruct((1, 1, places * LANES), f32),
            jax.ShapeDtypeStruct((nblk, LANES), f32),
            jax.ShapeDtypeStruct((nblk,), jnp.int32),
        ),
        in_specs=[SMEM] + [HBM] * 5,
        out_specs=(VMEM,) * 4,
        scratch_shapes=[
            pltpu.VMEM((3, segs), f32),
            pltpu.VMEM((3, segs), f32),
            pltpu.VMEM((2, slots), jnp.int32),
            pltpu.SMEM((nblk,), jnp.int32),
            pltpu.VMEM((LANES, LANES), f32),
            pltpu.VMEM((-(-6 * nblk // SUB) * SUB, LANES), f32),
            pltpu.VMEM((SUB, LANES), jnp.int32),
            pltpu.SemaphoreType.DMA((6,)),
        ],
        compiler_params=PARAMS,
        name="pack",
    )(
        pair_count,
        *(
            pltpu.with_memory_space_constraint(x, pltpu.HBM)
            for x in (block_cells, positions, burgers, pairs.T, mobility.reshape(nblk, LANES))
        ),
    )
    got = lax.all_to_all(load, ("slab", "dom"), 0, 0, tiled=True)
    below, above = neighbours(window, "slab")
    column = jnp.concatenate([below, window, above], axis=0)
    left, right = neighbours(column, "dom")
    left, column, right = (x.reshape(3 * places, 1, LANES) for x in (left, column, right))
    load2, vel, lists, coef, bur_wide, moved, old = pl.pallas_call(
        functools.partial(second_kernel, n_slab, n_dom, far_scale),
        out_shape=(
            payload,
            jax.ShapeDtypeStruct((3 * nblk, LANES), f32),
            jax.ShapeDtypeStruct((SUB, LANES), jnp.int32),
            jax.ShapeDtypeStruct((nblk * each, LANES, LANES), f32),
            wide,
            jax.ShapeDtypeStruct((3 * nblk, LANES), f32),
            jax.ShapeDtypeStruct((3 * nblk, LANES), f32),
        ),
        in_specs=[SMEM] + [VMEM] * 5,
        out_specs=(VMEM,) * 7,
        scratch_shapes=[pltpu.VMEM((LANES, LANES), f32), pltpu.VMEM((nblk, 3, LANES, LANES), f32)]
        + scratch
        + [
            pltpu.VMEM((9 * places, 1, LANES), f32),
            pltpu.VMEM((SUB, LANES), f32),
            pltpu.VMEM((SUB, LANES), f32),
            pltpu.VMEM((6 * nblk, LANES), f32),
            pltpu.VMEM((1, rows * LANES), f32),
            pltpu.SMEM((SUB, LANES), jnp.int32),
            pltpu.SMEM((SUB, LANES), f32),
            pltpu.SemaphoreType.DMA((2,)),
        ],
        compiler_params=PARAMS,
        name="step_one",
    )(cells, mob, got, left, column, right)
    got2 = lax.all_to_all(load2, ("slab", "dom"), 0, 0, tiled=True).reshape(ndev * rows, 1, LANES)
    return pl.pallas_call(
        functools.partial(third_kernel, n_slab, n_dom, far_scale),
        out_shape=(jax.ShapeDtypeStruct((3, segs), f32),) * 2,
        in_specs=[SMEM] + [VMEM] * 7,
        out_specs=(VMEM, VMEM),
        scratch_shapes=[pltpu.VMEM((nblk, 3, LANES, LANES), f32)] + scratch,
        compiler_params=PARAMS,
        name="step_two",
    )(lists, mob, vel, old, got2, coef, bur_wide, moved)


def solution(mesh):
    placed = (
        P(None, ("slab", "dom")),
        P(None, ("slab", "dom")),
        P(("slab", "dom")),
        P(("slab", "dom")),
        P(("slab", "dom"), None),
        P(("slab", "dom")),
    )
    return jax.shard_map(
        body,
        mesh=mesh,
        in_specs=placed,
        out_specs=(P(None, ("slab", "dom")), P(None, ("slab", "dom"))),
        check_vma=False,
    )
```

```python
import functools
import math

import jax
import jax.numpy as jnp
from jax import lax
from jax.experimental import pallas as pl
from jax.experimental.pallas import tpu as pltpu
from jax.sharding import PartitionSpec as P


LANES = 128
SUB = 8
CORE_NEAR = 0.25
CORE_FAR = 9.0
TIME_INCREMENT = 0.25
EXACT = lax.Precision.HIGHEST
VMEM = pl.BlockSpec(memory_space=pltpu.VMEM)
SMEM = pl.BlockSpec(memory_space=pltpu.SMEM)
HBM = pl.BlockSpec(memory_space=pltpu.HBM)
PARAMS = pltpu.CompilerParams(vmem_limit_bytes=8 * 1024 * 1024)
PARAMS_EVEN = pltpu.CompilerParams(vmem_limit_bytes=8 * 1024 * 1024)
SYM = ((0, 0), (0, 1), (0, 2), (1, 1), (1, 2), (2, 2))
MOMS = 3 + 9 + 18


def dot_lanes(a, b, precision=EXACT):
    return lax.dot_general(
        a, b, (((1,), (1,)), ((), ())), precision=precision, preferred_element_type=jnp.float32
    )


def center_of(cell):
    slab = jnp.floor(cell * 0.0625)
    rest = cell - 16.0 * slab
    row = jnp.floor(rest * 0.25)
    col = rest - 4.0 * row
    return (4.0 * slab + 2.0, 2.0 * row + 1.0, 2.0 * col + 1.0)


def put_cells(cells_smem, cell_ref):
    nblk = cells_smem.shape[0]
    lane = lax.broadcasted_iota(jnp.int32, (1, LANES), 1)
    last = jnp.zeros((1, LANES), jnp.float32)
    for b in range(nblk):
        cell = cells_smem[b].astype(jnp.float32)
        cell_ref[b : b + 1, :] = jnp.full((1, LANES), cell, jnp.float32)
        last = jnp.where(lane == MOMS * nblk + b, cell, last)
    cell_ref[nblk : nblk + 1, :] = last


def moment_row(pos, bur, cell_ref, stack_ref):
    nblk = pos[0].shape[0]
    z = center_of(cell_ref[0:nblk, :])
    d = [pos[k] - z[k] for k in range(3)]
    dd = [d[a] * d[e] for a, e in SYM]
    stack_ref[...] = jnp.zeros_like(stack_ref)
    m = 0
    for k in range(3):
        stack_ref[m * nblk : (m + 1) * nblk, :] = bur[k]
        m += 1
    for k in range(3):
        for a in range(3):
            stack_ref[m * nblk : (m + 1) * nblk, :] = bur[k] * d[a]
            m += 1
    for k in range(3):
        for j in range(6):
            stack_ref[m * nblk : (m + 1) * nblk, :] = bur[k] * dd[j]
            m += 1
    sums = dot_lanes(jnp.ones((SUB, LANES), jnp.float32), stack_ref[...])[0:1, :]
    lane = lax.broadcasted_iota(jnp.int32, (1, LANES), 1)
    return jnp.where(lane < MOMS * nblk, sums, cell_ref[nblk : nblk + 1, :])


def spread(out_ref, value):
    count = out_ref.shape[0]

    def put(d, carry):
        out_ref[d] = value
        return carry

    lax.fori_loop(0, count, put, 0, unroll=math.gcd(count, 32))


def first_kernel(
    count_ref, cells_hbm, pos_hbm, bur_hbm, pairs_hbm, mob_hbm,
    out_ref, win_ref, mob_ref, cell_ref,
    pos_ref, bur_ref, pairs_ref, cells_ref, stack_ref, load_ref, ids_ref, sem,
):
    moves = (
        (cells_hbm, cells_ref), (pos_hbm, pos_ref), (bur_hbm, bur_ref),
        (pairs_hbm, pairs_ref), (mob_hbm, mob_ref),
    )
    copies = [pltpu.make_async_copy(src, dst, sem.at[j]) for j, (src, dst) in enumerate(moves)]
    for copy in copies:
        copy.start()
    for copy in copies:
        copy.wait()
    nblk = cells_ref.shape[0]
    slots = pairs_ref.shape[1]
    pos, bur = [], []
    for k in range(3):
        for b in range(nblk):
            lanes = slice(b * LANES, (b + 1) * LANES)
            load_ref[k * nblk + b : k * nblk + b + 1, :] = pos_ref[k : k + 1, lanes]
            load_ref[(3 + k) * nblk + b : (3 + k) * nblk + b + 1, :] = bur_ref[k : k + 1, lanes]
    for k in range(3):
        pos.append(load_ref[k * nblk : (k + 1) * nblk, :])
        bur.append(load_ref[(3 + k) * nblk : (4 + k) * nblk, :])
    ids_ref[0:1, 0:slots] = pairs_ref[0:1, :]
    ids_ref[0:1, slots : 2 * slots] = pairs_ref[1:2, :]
    slot = lax.broadcasted_iota(jnp.int32, (1, LANES), 1)
    slot = jnp.where(slot < slots, slot, slot - slots)
    listed = jnp.where(slot < count_ref[0], ids_ref[0:1, :], -1).astype(jnp.float32)
    for r in range(6 * nblk):
        win_ref[0, :, r * LANES : (r + 1) * LANES] = load_ref[r : r + 1, :]
    win_ref[0, :, 6 * nblk * LANES :] = listed
    put_cells(cells_ref, cell_ref)
    spread(out_ref, moment_row(pos, bur, cell_ref, stack_ref))


def far_into(own_ref, bur_ref, mom_ref, center_ref, acc_ref, nblk, chunks):
    def visit(c, a, first):
        for t in range(LANES // SUB):
            rows = slice(t * SUB, (t + 1) * SUB)

            def mom(m):
                return mom_ref[c, m * nblk : m * nblk + 1, :]

            b = [bur_ref[a, k, rows, :] for k in range(3)]
            r = [own_ref[a, k, rows, :] - center_ref[c, k : k + 1, :] for k in range(3)]
            sq = r[0] * r[0] + r[1] * r[1] + (r[2] * r[2] + CORE_FAR)
            inv = lax.rsqrt(sq)
            inv2 = inv * inv
            inv3 = inv2 * inv
            q0 = b[0] * mom(0) + b[1] * mom(1) + b[2] * mom(2)
            q1 = [b[0] * mom(3 + e) + b[1] * mom(6 + e) + b[2] * mom(9 + e) for e in range(3)]
            q2 = [b[0] * mom(12 + j) + b[1] * mom(18 + j) + b[2] * mom(24 + j) for j in range(6)]
            u = [
                q2[0] * r[0] + q2[1] * r[1] + q2[2] * r[2],
                q2[1] * r[0] + q2[3] * r[1] + q2[4] * r[2],
                q2[2] * r[0] + q2[4] * r[1] + q2[5] * r[2],
            ]
            q1r = q1[0] * r[0] + q1[1] * r[1] + q1[2] * r[2]
            rqr = u[0] * r[0] + u[1] * r[1] + u[2] * r[2]
            trace = q2[0] + q2[3] + q2[5]
            inner = (3.0 * q1r - 0.5 * trace) + (2.5 * rqr) * inv2
            scal = q0 + inner * inv2
            for k in range(3):
                f = (r[k] * scal - (q1[k] + inv2 * u[k])) * inv3
                acc_ref[a, k, rows, :] = f if first else acc_ref[a, k, rows, :] + f

    def start(a, carry):
        visit(0, a, True)
        return carry

    def more(n, carry):
        visit(1 + n // nblk, n % nblk, False)
        return carry

    lax.fori_loop(0, nblk, start, 0)
    if chunks > 1:
        lax.fori_loop(0, nblk * (chunks - 1), more, 0)


def near_into(first_of, rows_at, coef_of, own_ref, used_of, acc_ref, nblk):
    for a in range(nblk):

        def ahead(n):
            return tuple(rows_at(first_of(a, 2 * n + j)) for j in range(2))

        def visit(n, carry):
            following = ahead(n + 1)
            p = [carry[j][:3] for j in range(2)]
            weigh = [coef_of(a, 2 * n + j, carry[j]) for j in range(2)]
            for t in range(LANES // SUB):
                rows = slice(t * SUB, (t + 1) * SUB)
                own = [own_ref[a, k, rows, :] for k in range(3)]
                f = []
                for j in range(2):
                    r = [own[k] - p[j][k] for k in range(3)]
                    sq = r[0] * r[0] + r[1] * r[1] + (r[2] * r[2] + CORE_NEAR)
                    u = lax.rsqrt(sq)
                    w = lax.rsqrt(sq + (CORE_FAR - CORE_NEAR))
                    wgt = weigh[j](t, rows) * (u * u * u - w * w * w)
                    f.append([wgt * r[k] for k in range(3)])
                for k in range(3):
                    acc_ref[a, k, rows, :] = acc_ref[a, k, rows, :] + (f[0][k] + f[1][k])
            return following

        lax.fori_loop(0, (used_of(a) + 1) // 2, visit, ahead(0))


def sum_lanes(acc_ref, force_ref, nblk):
    lane = lax.broadcasted_iota(jnp.int32, (SUB, LANES), 1)
    offset = lane - lax.broadcasted_iota(jnp.int32, (SUB, LANES), 0)
    for a in range(nblk):
        for k in range(3):
            out = jnp.zeros((SUB, LANES), jnp.float32)
            for t in range(LANES // SUB):
                total = jnp.sum(acc_ref[a, k, t * SUB : (t + 1) * SUB, :], axis=1, keepdims=True)
                out = jnp.where(offset == t * SUB, total, out)
            force_ref[k * nblk + a : k * nblk + a + 1, :] = jnp.sum(out, axis=0, keepdims=True)


def widen_own(row_of, own_ref, nblk):
    for a in range(nblk):
        for k in range(3):
            own_ref[a, k] = jnp.transpose(jnp.broadcast_to(row_of(k, a), (LANES, LANES)))


def window_ids(index, my_slab, my_dom, n_slab, n_dom, nblk):
    ids = jnp.full(index.shape, -2.0, jnp.float32)
    for k in range(9):
        s, e = my_slab + k % 3 - 1, my_dom + k // 3 - 1
        inside = (s >= 0) & (s < n_slab) & (e >= 0) & (e < n_dom)
        first = jnp.where(inside, (s * n_dom + e) * nblk - k * nblk, -100000)
        here = (index >= k * nblk) & (index < (k + 1) * nblk)
        ids = jnp.where(here, (index + first).astype(jnp.float32), ids)
    return ids


def build_lists(win_ref, rows, nblk, my_slab, my_dom, n_slab, n_dom, next_rows, count_ref, list_ref, mult_ref):
    high = -(-9 * nblk // SUB) * SUB
    place = (my_slab, my_dom, n_slab, n_dom, nblk)
    gid = window_ids(lax.broadcasted_iota(jnp.int32, (high, LANES), 0), *place)
    own = (my_slab * n_dom + my_dom) * nblk
    sub = lax.broadcasted_iota(jnp.int32, (SUB, LANES), 0)
    lane = lax.broadcasted_iota(jnp.int32, (SUB, LANES), 1)
    mine = jnp.where(sub < nblk, sub + own, -3).astype(jnp.float32)
    total = jnp.zeros((high, SUB), jnp.float32)
    for k in range(9):
        s, e = my_slab + k % 3 - 1, my_dom + k // 3 - 1
        inside = (s >= 0) & (s < n_slab) & (e >= 0) & (e < n_dom)
        row = jnp.where(inside, win_ref[k * rows + rows - 1], -1.0)
        other = pltpu.roll(row, LANES // 2, 1)
        left = (mine == row).astype(jnp.float32)
        right = (gid == other).astype(jnp.float32)
        total = total + dot_lanes(right, left, None)
    count_ref[...] = jnp.zeros_like(count_ref)
    count_ref[0:high, 0:SUB] = total
    count = jnp.transpose(count_ref[...])[0:SUB, :]
    met = jnp.where(count > 0.5, 1.0, 0.0)
    before = lax.broadcasted_iota(jnp.int32, (LANES, LANES), 0) < lax.broadcasted_iota(
        jnp.int32, (LANES, LANES), 1
    )
    rank = jnp.dot(met, before.astype(jnp.float32), preferred_element_type=jnp.float32)
    used = jnp.sum(met, axis=1, keepdims=True).astype(jnp.int32)
    list_ref[...] = jnp.where(lane == LANES - 1, used, 0)
    mult_ref[...] = jnp.zeros_like(mult_ref)
    line = window_ids(lane, *place)
    line = jnp.floor((line + 0.5) / nblk) * (next_rows - nblk) + line
    here = lane.astype(jnp.float32)
    here = jnp.floor((here + 0.5) / nblk) * (rows - nblk) + here
    spot = lax.broadcasted_iota(jnp.int32, (high, LANES), 0).astype(jnp.float32)
    line_high, here_high, count_high = (jnp.floor(x * 0.015625) for x in (line, here, count))
    line_low, here_low, count_low = line - 64.0 * line_high, here - 64.0 * here_high, count - 64.0 * count_high
    for a in range(nblk):
        pick = (rank[a : a + 1, :] == spot) & (met[a : a + 1, :] > 0.5)
        what = jnp.zeros((SUB, LANES), jnp.float32)
        parts = (line_high, line_low, here_high, here_low, count_high[a : a + 1, :], count_low[a : a + 1, :])
        for j, part in enumerate(parts):
            what = jnp.where(sub == j, part, what)
        out = dot_lanes(what, pick.astype(jnp.float32), None)
        list_ref[a : a + 1, 0:high] = (64.0 * out[0:1, :] + out[1:2, :] + 0.5).astype(jnp.int32)
        list_ref[nblk + a : nblk + a + 1, 0:high] = (64.0 * out[2:3, :] + out[3:4, :] + 0.5).astype(jnp.int32)
        mult_ref[a : a + 1, 0:high] = 64.0 * out[4:5, :] + out[5:6, :]


def gather_moments(got_ref, rows, mom_ref, center_ref, take_ref, nblk, ndev, far_scale):
    width = LANES // nblk
    for c in range(ndev // width):

        def take(d, carry):
            take_ref[pl.ds(d, 1), :] = got_ref[(c * width + d) * rows + rows - 1]
            return carry

        lax.fori_loop(0, width, take, 0, unroll=True)
        block = take_ref[...]
        turned = [block] + [pltpu.roll(block, LANES - b, 1) for b in range(1, nblk)]
        flat = jnp.transpose(jnp.concatenate(turned, axis=0))
        z = center_of(flat[MOMS * nblk : MOMS * nblk + 1, :])
        for k in range(3):
            center_ref[c, k : k + 1, :] = z[k]
        row = lax.broadcasted_iota(jnp.int32, (LANES, LANES), 0)
        mom_ref[c] = flat * jnp.where(row < 12 * nblk, far_scale, 3.0 * far_scale)


def second_kernel(
    n_slab, n_dom, far_scale,
    cell_ref, mob_ref, got_ref, low_ref, mid_ref, high_ref,
    own_ref, wide_ref,
    out_ref, vel_ref, list_ref, coef_ref, moved_ref, old_ref,
    stack_ref, acc_ref, force_ref, mom_ref, center_ref, take_ref,
    win_ref, count_ref, mult_ref, next_ref, flat_ref, list_smem, mult_smem, sem,
):
    nblk = mob_ref.shape[0]
    ndev = n_slab * n_dom
    rows = got_ref.shape[0] // ndev
    each = coef_ref.shape[0] // nblk
    my_slab, my_dom = lax.axis_index("slab"), lax.axis_index("dom")
    third = low_ref.shape[0]
    places = third // 3
    for j, ref in enumerate((low_ref, mid_ref, high_ref)):
        win_ref[j * third : (j + 1) * third] = ref[...]

    def own_row(k, b):
        return win_ref[4 * places + k * nblk + b]

    def own_bur(k, b):
        return own_row(3 + k, b)

    def first_of(a, e):
        return list_smem[nblk + a, e], mult_smem[a, e]

    def rows_at(found):
        first, mult = found
        rows = [win_ref[first + k * nblk] for k in range(6)]
        rows = rows[:3] + [row * mult for row in rows[3:]]
        return tuple(jnp.broadcast_to(row, (SUB, LANES)) for row in rows)

    def coef_of(a, e, found):
        def tile(t, rows):
            value = (
                wide_ref[a, 0, rows, :] * found[3]
                + wide_ref[a, 1, rows, :] * found[4]
                + wide_ref[a, 2, rows, :] * found[5]
            )
            coef_ref[a * each + e, rows, :] = value
            return value

        return tile

    build_lists(win_ref, places, nblk, my_slab, my_dom, n_slab, n_dom, 3 * nblk + 1, count_ref, list_ref, mult_ref)
    copies = [
        pltpu.make_async_copy(list_ref, list_smem, sem.at[0]),
        pltpu.make_async_copy(mult_ref, mult_smem, sem.at[1]),
    ]
    for copy in copies:
        copy.start()
    gather_moments(got_ref, rows, mom_ref, center_ref, take_ref, nblk, ndev, far_scale)
    far_into(own_ref, wide_ref, mom_ref, center_ref, acc_ref, nblk, mom_ref.shape[0])
    for copy in copies:
        copy.wait()
    near_into(first_of, rows_at, coef_of, own_ref, lambda a: list_smem[a, LANES - 1], acc_ref, nblk)
    sum_lanes(acc_ref, force_ref, nblk)
    pos, bur = [], []
    for k in range(3):
        here = slice(k * nblk, (k + 1) * nblk)
        vel = mob_ref[...] * force_ref[here, :]
        vel_ref[here, :] = vel
        for b in range(nblk):
            next_ref[k * nblk + b : k * nblk + b + 1, :] = own_row(k, b)
            next_ref[(3 + k) * nblk + b : (3 + k) * nblk + b + 1, :] = own_bur(k, b)
        old_ref[here, :] = next_ref[here, :]
        moved = next_ref[here, :] + TIME_INCREMENT * vel
        moved_ref[here, :] = moved
        pos.append(moved)
        bur.append(next_ref[(3 + k) * nblk : (4 + k) * nblk, :])
    last = moment_row(pos, bur, cell_ref, stack_ref)
    for r in range(3 * nblk):
        flat_ref[:, r * LANES : (r + 1) * LANES] = moved_ref[r : r + 1, :]
    flat_ref[:, 3 * nblk * LANES :] = last
    spread(out_ref, flat_ref[...])


def widen_kernel(row_ref, own_ref, wide_ref):
    nblk = own_ref.shape[0]
    widen_own(lambda k, b: row_ref[k * nblk + b], own_ref, nblk)
    widen_own(lambda k, b: row_ref[(3 + k) * nblk + b], wide_ref, nblk)


def third_kernel(
    n_slab, n_dom, far_scale,
    list_ref, mob_ref, vel_ref, old_ref, got_ref, coef_ref, wide_ref, next_ref,
    moved_ref, velocity_ref,
    own_ref, acc_ref, force_ref, mom_ref, center_ref, take_ref, list_smem, sem,
):
    copy = pltpu.make_async_copy(list_ref, list_smem, sem)
    copy.start()
    nblk = mob_ref.shape[0]
    ndev = n_slab * n_dom
    rows = got_ref.shape[0] // ndev
    each = coef_ref.shape[0] // nblk

    def first_of(a, e):
        return list_smem[a, e]

    def rows_at(first):
        return tuple(jnp.broadcast_to(got_ref[first + k * nblk], (SUB, LANES)) for k in range(3))

    def coef_of(a, e, found):
        return lambda t, rows: coef_ref[a * each + e, rows, :]

    widen_own(lambda k, b: next_ref[k * nblk + b : k * nblk + b + 1, :], own_ref, nblk)
    gather_moments(got_ref, rows, mom_ref, center_ref, take_ref, nblk, ndev, far_scale)
    far_into(own_ref, wide_ref, mom_ref, center_ref, acc_ref, nblk, mom_ref.shape[0])
    copy.wait()
    near_into(first_of, rows_at, coef_of, own_ref, lambda a: list_smem[a, LANES - 1], acc_ref, nblk)
    sum_lanes(acc_ref, force_ref, nblk)
    for k in range(3):
        here = slice(k * nblk, (k + 1) * nblk)
        force_ref[here, :] = 0.5 * (vel_ref[here, :] + mob_ref[...] * force_ref[here, :])
        for b in range(nblk):
            lanes = slice(b * LANES, (b + 1) * LANES)
            mean = force_ref[k * nblk + b : k * nblk + b + 1, :]
            velocity_ref[k : k + 1, lanes] = mean
            moved_ref[k : k + 1, lanes] = old_ref[k * nblk + b : k * nblk + b + 1, :] + TIME_INCREMENT * mean


def neighbours(x, axis):
    count = lax.axis_size(axis)
    below = lax.ppermute(x, axis, [(i, (i + 1) % count) for i in range(count)])
    above = lax.ppermute(x, axis, [((i + 1) % count, i) for i in range(count)])
    return below, above


def body(positions, burgers, mobility, block_cells, pairs, pair_count):
    f32 = jnp.float32
    segs = positions.shape[1]
    nblk = block_cells.shape[0]
    slots = pairs.shape[0]
    n_slab, n_dom = lax.axis_size("slab"), lax.axis_size("dom")
    ndev = n_slab * n_dom
    far_scale = math.sqrt(16 * n_slab / (segs * ndev))
    rows, places = 3 * nblk + 1, 6 * nblk + 1
    each = 9 * nblk + 2
    chunks = ndev * nblk // LANES
    high = -(-(3 * nblk) // SUB) * SUB
    wide = jax.ShapeDtypeStruct((nblk, 3, LANES, LANES), f32)
    payload = jax.ShapeDtypeStruct((ndev, 1, rows * LANES), f32)
    scratch = [
        pltpu.VMEM((nblk, 3, LANES, LANES), f32),
        pltpu.VMEM((high, LANES), f32),
        pltpu.VMEM((chunks, LANES, LANES), f32),
        pltpu.VMEM((chunks, SUB, LANES), f32),
        pltpu.VMEM((LANES // nblk, LANES), f32),
    ]
    load, window, mob, cells = pl.pallas_call(
        first_kernel,
        out_shape=(
            jax.ShapeDtypeStruct((ndev, 1, LANES), f32),
            jax.ShapeDtypeStruct((1, 1, places * LANES), f32),
            jax.ShapeDtypeStruct((nblk, LANES), f32),
            jax.ShapeDtypeStruct((SUB, LANES), f32),
        ),
        in_specs=[SMEM] + [HBM] * 5,
        out_specs=(VMEM,) * 4,
        scratch_shapes=[
            pltpu.VMEM((3, segs), f32),
            pltpu.VMEM((3, segs), f32),
            pltpu.VMEM((2, slots), jnp.int32),
            pltpu.SMEM((nblk,), jnp.int32),
            pltpu.VMEM((LANES, LANES), f32),
            pltpu.VMEM((-(-6 * nblk // SUB) * SUB, LANES), f32),
            pltpu.VMEM((SUB, LANES), jnp.int32),
            pltpu.SemaphoreType.DMA((5,)),
        ],
        compiler_params=PARAMS,
        name="pack",
    )(
        pair_count,
        *(
            pltpu.with_memory_space_constraint(x, pltpu.HBM)
            for x in (block_cells, positions, burgers, pairs.T, mobility.reshape(nblk, LANES))
        ),
    )
    got = lax.all_to_all(load, ("slab", "dom"), 0, 0, tiled=True)
    below, above = neighbours(window, "slab")
    column = jnp.concatenate([below, window, above], axis=0)
    left, right = neighbours(column, "dom")
    left, column, right = (x.reshape(3 * places, 1, LANES) for x in (left, column, right))
    pos_wide, bur_wide = pl.pallas_call(
        widen_kernel,
        out_shape=(wide, wide),
        in_specs=[VMEM],
        out_specs=(VMEM, VMEM),
        compiler_params=PARAMS,
        name="widen",
    )(window.reshape(places, 1, LANES))
    load2, vel, lists, coef, moved, old = pl.pallas_call(
        functools.partial(second_kernel, n_slab, n_dom, far_scale),
        out_shape=(
            payload,
            jax.ShapeDtypeStruct((3 * nblk, LANES), f32),
            jax.ShapeDtypeStruct((SUB, LANES), jnp.int32),
            jax.ShapeDtypeStruct((nblk * each, LANES, LANES), f32),
            jax.ShapeDtypeStruct((3 * nblk, LANES), f32),
            jax.ShapeDtypeStruct((3 * nblk, LANES), f32),
        ),
        in_specs=[VMEM] * 8,
        out_specs=(VMEM,) * 6,
        scratch_shapes=[pltpu.VMEM((LANES, LANES), f32)]
        + scratch
        + [
            pltpu.VMEM((9 * places, 1, LANES), f32),
            pltpu.VMEM((LANES, LANES), f32),
            pltpu.VMEM((SUB, LANES), f32),
            pltpu.VMEM((6 * nblk, LANES), f32),
            pltpu.VMEM((1, rows * LANES), f32),
            pltpu.SMEM((SUB, LANES), jnp.int32),
            pltpu.SMEM((SUB, LANES), f32),
            pltpu.SemaphoreType.DMA((2,)),
        ],
        compiler_params=PARAMS,
        name="step_one",
    )(cells, mob, got, left, column, right, pos_wide, bur_wide)
    got2 = lax.all_to_all(load2, ("slab", "dom"), 0, 0, tiled=True).reshape(ndev * rows, 1, LANES)
    return pl.pallas_call(
        functools.partial(third_kernel, n_slab, n_dom, far_scale),
        out_shape=(jax.ShapeDtypeStruct((3, segs), f32),) * 2,
        in_specs=[VMEM] * 8,
        out_specs=(VMEM, VMEM),
        scratch_shapes=[pltpu.VMEM((nblk, 3, LANES, LANES), f32)]
        + scratch
        + [pltpu.SMEM((SUB, LANES), jnp.int32), pltpu.SemaphoreType.DMA(())],
        compiler_params=PARAMS_EVEN,
        name="step_two",
    )(lists, mob, vel, old, got2, coef, bur_wide, moved)


def solution(mesh):
    placed = (
        P(None, ("slab", "dom")),
        P(None, ("slab", "dom")),
        P(("slab", "dom")),
        P(("slab", "dom")),
        P(("slab", "dom"), None),
        P(("slab", "dom")),
    )
    return jax.shard_map(
        body,
        mesh=mesh,
        in_specs=placed,
        out_specs=(P(None, ("slab", "dom")), P(None, ("slab", "dom"))),
        check_vma=False,
    )
```

```python
import functools
import math

import jax
import jax.numpy as jnp
from jax import lax
from jax.experimental import pallas as pl
from jax.experimental.pallas import tpu as pltpu
from jax.sharding import PartitionSpec as P


LANES = 128
SUB = 8
CORE_NEAR = 0.25
CORE_FAR = 9.0
TIME_INCREMENT = 0.25
EXACT = lax.Precision.HIGHEST
VMEM = pl.BlockSpec(memory_space=pltpu.VMEM)
SMEM = pl.BlockSpec(memory_space=pltpu.SMEM)
HBM = pl.BlockSpec(memory_space=pltpu.HBM)
PARAMS = pltpu.CompilerParams(vmem_limit_bytes=8 * 1024 * 1024)
PARAMS_EVEN = pltpu.CompilerParams(vmem_limit_bytes=8 * 1024 * 1024)
SYM = ((0, 0), (0, 1), (0, 2), (1, 1), (1, 2), (2, 2))
MOMS = 3 + 9 + 18


def dot_lanes(a, b, precision=EXACT):
    return lax.dot_general(
        a, b, (((1,), (1,)), ((), ())), precision=precision, preferred_element_type=jnp.float32
    )


def center_of(cell):
    slab = jnp.floor(cell * 0.0625)
    rest = cell - 16.0 * slab
    row = jnp.floor(rest * 0.25)
    col = rest - 4.0 * row
    return (4.0 * slab + 2.0, 2.0 * row + 1.0, 2.0 * col + 1.0)


def put_cells(cells_smem, cell_ref):
    nblk = cells_smem.shape[0]
    lane = lax.broadcasted_iota(jnp.int32, (1, LANES), 1)
    last = jnp.zeros((1, LANES), jnp.float32)
    for b in range(nblk):
        cell = cells_smem[b].astype(jnp.float32)
        cell_ref[b : b + 1, :] = jnp.full((1, LANES), cell, jnp.float32)
        last = jnp.where(lane == MOMS * nblk + b, cell, last)
    cell_ref[nblk : nblk + 1, :] = last


def moment_row(pos, bur, cell_ref, stack_ref):
    nblk = pos[0].shape[0]
    z = center_of(cell_ref[0:nblk, :])
    d = [pos[k] - z[k] for k in range(3)]
    dd = [d[a] * d[e] for a, e in SYM]
    stack_ref[...] = jnp.zeros_like(stack_ref)
    m = 0
    for k in range(3):
        stack_ref[m * nblk : (m + 1) * nblk, :] = bur[k]
        m += 1
    for k in range(3):
        for a in range(3):
            stack_ref[m * nblk : (m + 1) * nblk, :] = bur[k] * d[a]
            m += 1
    for k in range(3):
        for j in range(6):
            stack_ref[m * nblk : (m + 1) * nblk, :] = bur[k] * dd[j]
            m += 1
    sums = dot_lanes(jnp.ones((SUB, LANES), jnp.float32), stack_ref[...])[0:1, :]
    lane = lax.broadcasted_iota(jnp.int32, (1, LANES), 1)
    return jnp.where(lane < MOMS * nblk, sums, cell_ref[nblk : nblk + 1, :])


def spread(out_ref, value):
    count = out_ref.shape[0]

    def put(d, carry):
        out_ref[d] = value
        return carry

    lax.fori_loop(0, count, put, 0, unroll=math.gcd(count, 32))


def first_kernel(
    count_ref, cells_hbm, pos_hbm, bur_hbm, pairs_hbm, mob_hbm,
    out_ref, win_ref, mob_ref, cell_ref,
    pos_ref, bur_ref, pairs_ref, cells_ref, stack_ref, load_ref, ids_ref, sem,
):
    moves = (
        (cells_hbm, cells_ref), (pos_hbm, pos_ref), (bur_hbm, bur_ref),
        (pairs_hbm, pairs_ref), (mob_hbm, mob_ref),
    )
    copies = [pltpu.make_async_copy(src, dst, sem.at[j]) for j, (src, dst) in enumerate(moves)]
    for copy in copies:
        copy.start()
    for copy in copies:
        copy.wait()
    nblk = cells_ref.shape[0]
    slots = pairs_ref.shape[1]
    pos, bur = [], []
    for k in range(3):
        for b in range(nblk):
            lanes = slice(b * LANES, (b + 1) * LANES)
            load_ref[k * nblk + b : k * nblk + b + 1, :] = pos_ref[k : k + 1, lanes]
            load_ref[(3 + k) * nblk + b : (3 + k) * nblk + b + 1, :] = bur_ref[k : k + 1, lanes]
    for k in range(3):
        pos.append(load_ref[k * nblk : (k + 1) * nblk, :])
        bur.append(load_ref[(3 + k) * nblk : (4 + k) * nblk, :])
    ids_ref[0:1, 0:slots] = pairs_ref[0:1, :]
    ids_ref[0:1, slots : 2 * slots] = pairs_ref[1:2, :]
    slot = lax.broadcasted_iota(jnp.int32, (1, LANES), 1)
    slot = jnp.where(slot < slots, slot, slot - slots)
    listed = jnp.where(slot < count_ref[0], ids_ref[0:1, :], -1).astype(jnp.float32)
    for r in range(6 * nblk):
        win_ref[0, :, r * LANES : (r + 1) * LANES] = load_ref[r : r + 1, :]
    win_ref[0, :, 6 * nblk * LANES :] = listed
    put_cells(cells_ref, cell_ref)
    spread(out_ref, moment_row(pos, bur, cell_ref, stack_ref))


def far_into(own_ref, bur_ref, mom_ref, center_ref, acc_ref, nblk, chunks):
    def visit(c, a, first):
        for t in range(LANES // SUB):
            rows = slice(t * SUB, (t + 1) * SUB)

            def mom(m):
                return mom_ref[c, m * nblk : m * nblk + 1, :]

            b = [bur_ref[a, k, rows, :] for k in range(3)]
            r = [own_ref[a, k, rows, :] - center_ref[c, k : k + 1, :] for k in range(3)]
            sq = r[0] * r[0] + r[1] * r[1] + (r[2] * r[2] + CORE_FAR)
            inv = lax.rsqrt(sq)
            inv2 = inv * inv
            inv3 = inv2 * inv
            q0 = b[0] * mom(0) + b[1] * mom(1) + b[2] * mom(2)
            q1 = [b[0] * mom(3 + e) + b[1] * mom(6 + e) + b[2] * mom(9 + e) for e in range(3)]
            q2 = [b[0] * mom(12 + j) + b[1] * mom(18 + j) + b[2] * mom(24 + j) for j in range(6)]
            u = [
                q2[0] * r[0] + q2[1] * r[1] + q2[2] * r[2],
                q2[1] * r[0] + q2[3] * r[1] + q2[4] * r[2],
                q2[2] * r[0] + q2[4] * r[1] + q2[5] * r[2],
            ]
            q1r = q1[0] * r[0] + q1[1] * r[1] + q1[2] * r[2]
            rqr = u[0] * r[0] + u[1] * r[1] + u[2] * r[2]
            trace = q2[0] + q2[3] + q2[5]
            inner = (3.0 * q1r - 0.5 * trace) + (2.5 * rqr) * inv2
            scal = q0 + inner * inv2
            for k in range(3):
                f = (r[k] * scal - (q1[k] + inv2 * u[k])) * inv3
                acc_ref[a, k, rows, :] = f if first else acc_ref[a, k, rows, :] + f

    def start(a, carry):
        visit(0, a, True)
        return carry

    def more(n, carry):
        visit(1 + n // nblk, n % nblk, False)
        return carry

    lax.fori_loop(0, nblk, start, 0)
    if chunks > 1:
        lax.fori_loop(0, nblk * (chunks - 1), more, 0)


def near_into(first_of, rows_at, coef_of, own_ref, used_of, acc_ref, nblk):
    def ahead(a, n):
        return tuple(rows_at(first_of(a, 2 * n + j)) for j in range(2))

    def add(a, n, found):
        weigh = [coef_of(a, 2 * n + j, rows) for j, rows in enumerate(found)]
        for t in range(LANES // SUB):
            rows = slice(t * SUB, (t + 1) * SUB)
            own = [own_ref[a, k, rows, :] for k in range(3)]
            f = [None] * 3
            for j, other in enumerate(found):
                r = [own[k] - other[k] for k in range(3)]
                sq = r[0] * r[0] + r[1] * r[1] + (r[2] * r[2] + CORE_NEAR)
                u = lax.rsqrt(sq)
                w = lax.rsqrt(sq + (CORE_FAR - CORE_NEAR))
                wgt = weigh[j](t, rows) * (u * u * u - w * w * w)
                f = [wgt * r[k] if f[k] is None else f[k] + wgt * r[k] for k in range(3)]
            for k in range(3):
                acc_ref[a, k, rows, :] = acc_ref[a, k, rows, :] + f[k]

    for a in range(nblk):
        used = used_of(a)

        def visit(n, carry):
            following = ahead(a, n + 1)
            add(a, n, carry)
            return following

        def last(n, carry):
            add(a, n, carry[:1])
            return carry

        turns = used // 2
        rest = lax.fori_loop(0, turns, visit, ahead(a, 0))
        lax.fori_loop(turns, turns + used % 2, last, rest)


def sum_lanes(acc_ref, force_ref, nblk):
    lane = lax.broadcasted_iota(jnp.int32, (SUB, LANES), 1)
    offset = lane - lax.broadcasted_iota(jnp.int32, (SUB, LANES), 0)
    for a in range(nblk):
        for k in range(3):
            out = jnp.zeros((SUB, LANES), jnp.float32)
            for t in range(LANES // SUB):
                total = jnp.sum(acc_ref[a, k, t * SUB : (t + 1) * SUB, :], axis=1, keepdims=True)
                out = jnp.where(offset == t * SUB, total, out)
            force_ref[k * nblk + a : k * nblk + a + 1, :] = jnp.sum(out, axis=0, keepdims=True)


def widen_own(row_of, own_ref, nblk):
    for a in range(nblk):
        for k in range(3):
            own_ref[a, k] = jnp.transpose(jnp.broadcast_to(row_of(k, a), (LANES, LANES)))


def window_ids(index, my_slab, my_dom, n_slab, n_dom, nblk):
    ids = jnp.full(index.shape, -2.0, jnp.float32)
    for k in range(9):
        s, e = my_slab + k // 3 - 1, my_dom + k % 3 - 1
        inside = (s >= 0) & (s < n_slab) & (e >= 0) & (e < n_dom)
        first = jnp.where(inside, (s * n_dom + e) * nblk - k * nblk, -100000)
        here = (index >= k * nblk) & (index < (k + 1) * nblk)
        ids = jnp.where(here, (index + first).astype(jnp.float32), ids)
    return ids


def build_lists(win_ref, rows, nblk, my_slab, my_dom, n_slab, n_dom, next_rows, count_ref, list_ref, mult_ref):
    high = -(-9 * nblk // SUB) * SUB
    place = (my_slab, my_dom, n_slab, n_dom, nblk)
    gid = window_ids(lax.broadcasted_iota(jnp.int32, (high, LANES), 0), *place)
    own = (my_slab * n_dom + my_dom) * nblk
    sub = lax.broadcasted_iota(jnp.int32, (SUB, LANES), 0)
    lane = lax.broadcasted_iota(jnp.int32, (SUB, LANES), 1)
    mine = jnp.where(sub < nblk, sub + own, -3).astype(jnp.float32)
    total = jnp.zeros((high, SUB), jnp.float32)
    for k in range(9):
        s, e = my_slab + k // 3 - 1, my_dom + k % 3 - 1
        inside = (s >= 0) & (s < n_slab) & (e >= 0) & (e < n_dom)
        row = jnp.where(inside, win_ref[k * rows + rows - 1], -1.0)
        other = pltpu.roll(row, LANES // 2, 1)
        left = (mine == row).astype(jnp.float32)
        right = (gid == other).astype(jnp.float32)
        total = total + dot_lanes(right, left, None)
    count_ref[...] = jnp.zeros_like(count_ref)
    count_ref[0:high, 0:SUB] = total
    count = jnp.transpose(count_ref[...])[0:SUB, :]
    met = jnp.where(count > 0.5, 1.0, 0.0)
    before = lax.broadcasted_iota(jnp.int32, (LANES, LANES), 0) < lax.broadcasted_iota(
        jnp.int32, (LANES, LANES), 1
    )
    rank = jnp.dot(met, before.astype(jnp.float32), preferred_element_type=jnp.float32)
    used = jnp.sum(met, axis=1, keepdims=True).astype(jnp.int32)
    list_ref[...] = jnp.where(lane == LANES - 1, used, 0)
    mult_ref[...] = jnp.zeros_like(mult_ref)
    line = window_ids(lane, *place)
    line = jnp.floor((line + 0.5) / nblk) * (next_rows - nblk) + line
    here = lane.astype(jnp.float32)
    here = jnp.floor((here + 0.5) / nblk) * (rows - nblk) + here
    spot = lax.broadcasted_iota(jnp.int32, (high, LANES), 0).astype(jnp.float32)
    line_high, here_high, count_high = (jnp.floor(x * 0.015625) for x in (line, here, count))
    line_low, here_low, count_low = line - 64.0 * line_high, here - 64.0 * here_high, count - 64.0 * count_high
    for a in range(nblk):
        pick = (rank[a : a + 1, :] == spot) & (met[a : a + 1, :] > 0.5)
        what = jnp.zeros((SUB, LANES), jnp.float32)
        parts = (line_high, line_low, here_high, here_low, count_high[a : a + 1, :], count_low[a : a + 1, :])
        for j, part in enumerate(parts):
            what = jnp.where(sub == j, part, what)
        out = dot_lanes(what, pick.astype(jnp.float32), None)
        list_ref[a : a + 1, 0:high] = (64.0 * out[0:1, :] + out[1:2, :] + 0.5).astype(jnp.int32)
        list_ref[nblk + a : nblk + a + 1, 0:high] = (64.0 * out[2:3, :] + out[3:4, :] + 0.5).astype(jnp.int32)
        mult_ref[a : a + 1, 0:high] = 64.0 * out[4:5, :] + out[5:6, :]


def gather_moments(got_ref, rows, mom_ref, center_ref, take_ref, nblk, ndev, far_scale):
    width = LANES // nblk
    for c in range(ndev // width):

        def take(d, carry):
            take_ref[pl.ds(d, 1), :] = got_ref[(c * width + d) * rows + rows - 1]
            return carry

        lax.fori_loop(0, width, take, 0, unroll=True)
        block = take_ref[...]
        turned = [block] + [pltpu.roll(block, LANES - b, 1) for b in range(1, nblk)]
        flat = jnp.transpose(jnp.concatenate(turned, axis=0))
        z = center_of(flat[MOMS * nblk : MOMS * nblk + 1, :])
        for k in range(3):
            center_ref[c, k : k + 1, :] = z[k]
        row = lax.broadcasted_iota(jnp.int32, (LANES, LANES), 0)
        mom_ref[c] = flat * jnp.where(row < 12 * nblk, far_scale, 3.0 * far_scale)


def second_kernel(
    n_slab, n_dom, far_scale,
    cell_ref, mob_ref, got_ref, low_ref, mid_ref, high_ref,
    own_ref, wide_ref,
    out_ref, vel_ref, list_ref, coef_ref, moved_ref, old_ref,
    stack_ref, acc_ref, force_ref, mom_ref, center_ref, take_ref,
    win_ref, count_ref, mult_ref, next_ref, flat_ref, list_smem, mult_smem, sem,
):
    nblk = mob_ref.shape[0]
    ndev = n_slab * n_dom
    rows = got_ref.shape[0] // ndev
    each = coef_ref.shape[0] // nblk
    my_slab, my_dom = lax.axis_index("slab"), lax.axis_index("dom")
    third = low_ref.shape[0]
    places = third // 3
    for j, ref in enumerate((low_ref, mid_ref, high_ref)):
        win_ref[j * third : (j + 1) * third] = ref[...]

    def own_row(k, b):
        return win_ref[4 * places + k * nblk + b]

    def own_bur(k, b):
        return own_row(3 + k, b)

    def first_of(a, e):
        return list_smem[nblk + a, e], mult_smem[a, e]

    def rows_at(found):
        first, mult = found
        rows = [win_ref[first + k * nblk] for k in range(6)]
        rows = rows[:3] + [row * mult for row in rows[3:]]
        return tuple(jnp.broadcast_to(row, (SUB, LANES)) for row in rows)

    def coef_of(a, e, found):
        def tile(t, rows):
            value = (
                wide_ref[a, 0, rows, :] * found[3]
                + wide_ref[a, 1, rows, :] * found[4]
                + wide_ref[a, 2, rows, :] * found[5]
            )
            coef_ref[a * each + e, rows, :] = value
            return value

        return tile

    build_lists(win_ref, places, nblk, my_slab, my_dom, n_slab, n_dom, 3 * nblk + 1, count_ref, list_ref, mult_ref)
    copies = [
        pltpu.make_async_copy(list_ref, list_smem, sem.at[0]),
        pltpu.make_async_copy(mult_ref, mult_smem, sem.at[1]),
    ]
    for copy in copies:
        copy.start()
    gather_moments(got_ref, rows, mom_ref, center_ref, take_ref, nblk, ndev, far_scale)
    far_into(own_ref, wide_ref, mom_ref, center_ref, acc_ref, nblk, mom_ref.shape[0])
    for copy in copies:
        copy.wait()
    near_into(first_of, rows_at, coef_of, own_ref, lambda a: list_smem[a, LANES - 1], acc_ref, nblk)
    sum_lanes(acc_ref, force_ref, nblk)
    pos, bur = [], []
    for k in range(3):
        here = slice(k * nblk, (k + 1) * nblk)
        vel = mob_ref[...] * force_ref[here, :]
        vel_ref[here, :] = vel
        for b in range(nblk):
            next_ref[k * nblk + b : k * nblk + b + 1, :] = own_row(k, b)
            next_ref[(3 + k) * nblk + b : (3 + k) * nblk + b + 1, :] = own_bur(k, b)
        old_ref[here, :] = next_ref[here, :]
        moved = next_ref[here, :] + TIME_INCREMENT * vel
        moved_ref[here, :] = moved
        pos.append(moved)
        bur.append(next_ref[(3 + k) * nblk : (4 + k) * nblk, :])
    last = moment_row(pos, bur, cell_ref, stack_ref)
    for r in range(3 * nblk):
        flat_ref[:, r * LANES : (r + 1) * LANES] = moved_ref[r : r + 1, :]
    flat_ref[:, 3 * nblk * LANES :] = last
    spread(out_ref, flat_ref[...])


def widen_kernel(row_ref, own_ref, wide_ref):
    nblk = own_ref.shape[0]
    widen_own(lambda k, b: row_ref[k * nblk + b], own_ref, nblk)
    widen_own(lambda k, b: row_ref[(3 + k) * nblk + b], wide_ref, nblk)


def third_kernel(
    n_slab, n_dom, far_scale,
    list_ref, mob_ref, vel_ref, old_ref, got_ref, coef_ref, wide_ref, next_ref,
    moved_ref, velocity_ref,
    own_ref, acc_ref, force_ref, mom_ref, center_ref, take_ref, list_smem, sem,
):
    copy = pltpu.make_async_copy(list_ref, list_smem, sem)
    copy.start()
    nblk = mob_ref.shape[0]
    ndev = n_slab * n_dom
    rows = got_ref.shape[0] // ndev
    each = coef_ref.shape[0] // nblk

    def first_of(a, e):
        return list_smem[a, e]

    def rows_at(first):
        return tuple(jnp.broadcast_to(got_ref[first + k * nblk], (SUB, LANES)) for k in range(3))

    def coef_of(a, e, found):
        return lambda t, rows: coef_ref[a * each + e, rows, :]

    widen_own(lambda k, b: next_ref[k * nblk + b : k * nblk + b + 1, :], own_ref, nblk)
    gather_moments(got_ref, rows, mom_ref, center_ref, take_ref, nblk, ndev, far_scale)
    far_into(own_ref, wide_ref, mom_ref, center_ref, acc_ref, nblk, mom_ref.shape[0])
    copy.wait()
    near_into(first_of, rows_at, coef_of, own_ref, lambda a: list_smem[a, LANES - 1], acc_ref, nblk)
    sum_lanes(acc_ref, force_ref, nblk)
    for k in range(3):
        here = slice(k * nblk, (k + 1) * nblk)
        force_ref[here, :] = 0.5 * (vel_ref[here, :] + mob_ref[...] * force_ref[here, :])
        for b in range(nblk):
            lanes = slice(b * LANES, (b + 1) * LANES)
            mean = force_ref[k * nblk + b : k * nblk + b + 1, :]
            velocity_ref[k : k + 1, lanes] = mean
            moved_ref[k : k + 1, lanes] = old_ref[k * nblk + b : k * nblk + b + 1, :] + TIME_INCREMENT * mean


def neighbours(x, axis):
    count = lax.axis_size(axis)
    above = lax.ppermute(x, axis, [((i + 1) % count, i) for i in range(count)])
    below = lax.ppermute(x, axis, [(i, (i + 1) % count) for i in range(count)])
    return below, above


def body(positions, burgers, mobility, block_cells, pairs, pair_count):
    f32 = jnp.float32
    segs = positions.shape[1]
    nblk = block_cells.shape[0]
    slots = pairs.shape[0]
    n_slab, n_dom = lax.axis_size("slab"), lax.axis_size("dom")
    ndev = n_slab * n_dom
    far_scale = math.sqrt(16 * n_slab / (segs * ndev))
    rows, places = 3 * nblk + 1, 6 * nblk + 1
    each = 9 * nblk + 2
    chunks = ndev * nblk // LANES
    high = -(-(3 * nblk) // SUB) * SUB
    wide = jax.ShapeDtypeStruct((nblk, 3, LANES, LANES), f32)
    payload = jax.ShapeDtypeStruct((ndev, 1, rows * LANES), f32)
    scratch = [
        pltpu.VMEM((nblk, 3, LANES, LANES), f32),
        pltpu.VMEM((high, LANES), f32),
        pltpu.VMEM((chunks, LANES, LANES), f32),
        pltpu.VMEM((chunks, SUB, LANES), f32),
        pltpu.VMEM((LANES // nblk, LANES), f32),
    ]
    load, window, mob, cells = pl.pallas_call(
        first_kernel,
        out_shape=(
            jax.ShapeDtypeStruct((ndev, 1, LANES), f32),
            jax.ShapeDtypeStruct((1, 1, places * LANES), f32),
            jax.ShapeDtypeStruct((nblk, LANES), f32),
            jax.ShapeDtypeStruct((SUB, LANES), f32),
        ),
        in_specs=[SMEM] + [HBM] * 5,
        out_specs=(VMEM,) * 4,
        scratch_shapes=[
            pltpu.VMEM((3, segs), f32),
            pltpu.VMEM((3, segs), f32),
            pltpu.VMEM((2, slots), jnp.int32),
            pltpu.SMEM((nblk,), jnp.int32),
            pltpu.VMEM((LANES, LANES), f32),
            pltpu.VMEM((-(-6 * nblk // SUB) * SUB, LANES), f32),
            pltpu.VMEM((SUB, LANES), jnp.int32),
            pltpu.SemaphoreType.DMA((5,)),
        ],
        compiler_params=PARAMS,
        name="pack",
    )(
        pair_count,
        *(
            pltpu.with_memory_space_constraint(x, pltpu.HBM)
            for x in (block_cells, positions, burgers, pairs.T, mobility.reshape(nblk, LANES))
        ),
    )
    got = lax.all_to_all(load, ("slab", "dom"), 0, 0, tiled=True)
    below, above = neighbours(window, "dom")
    row = jnp.concatenate([below, window, above], axis=0)
    left, right = neighbours(row, "slab")
    left, row, right = (x.reshape(3 * places, 1, LANES) for x in (left, row, right))
    pos_wide, bur_wide = pl.pallas_call(
        widen_kernel,
        out_shape=(wide, wide),
        in_specs=[VMEM],
        out_specs=(VMEM, VMEM),
        compiler_params=PARAMS,
        name="widen",
    )(window.reshape(places, 1, LANES))
    load2, vel, lists, coef, moved, old = pl.pallas_call(
        functools.partial(second_kernel, n_slab, n_dom, far_scale),
        out_shape=(
            payload,
            jax.ShapeDtypeStruct((3 * nblk, LANES), f32),
            jax.ShapeDtypeStruct((SUB, LANES), jnp.int32),
            jax.ShapeDtypeStruct((nblk * each, LANES, LANES), f32),
            jax.ShapeDtypeStruct((3 * nblk, LANES), f32),
            jax.ShapeDtypeStruct((3 * nblk, LANES), f32),
        ),
        in_specs=[VMEM] * 8,
        out_specs=(VMEM,) * 6,
        scratch_shapes=[pltpu.VMEM((LANES, LANES), f32)]
        + scratch
        + [
            pltpu.VMEM((9 * places, 1, LANES), f32),
            pltpu.VMEM((LANES, LANES), f32),
            pltpu.VMEM((SUB, LANES), f32),
            pltpu.VMEM((6 * nblk, LANES), f32),
            pltpu.VMEM((1, rows * LANES), f32),
            pltpu.SMEM((SUB, LANES), jnp.int32),
            pltpu.SMEM((SUB, LANES), f32),
            pltpu.SemaphoreType.DMA((2,)),
        ],
        compiler_params=PARAMS,
        name="step_one",
    )(cells, mob, got, left, row, right, pos_wide, bur_wide)
    got2 = lax.all_to_all(load2, ("slab", "dom"), 0, 0, tiled=True).reshape(ndev * rows, 1, LANES)
    return pl.pallas_call(
        functools.partial(third_kernel, n_slab, n_dom, far_scale),
        out_shape=(jax.ShapeDtypeStruct((3, segs), f32),) * 2,
        in_specs=[VMEM] * 8,
        out_specs=(VMEM, VMEM),
        scratch_shapes=[pltpu.VMEM((nblk, 3, LANES, LANES), f32)]
        + scratch
        + [pltpu.SMEM((SUB, LANES), jnp.int32), pltpu.SemaphoreType.DMA(())],
        compiler_params=PARAMS_EVEN,
        name="step_two",
    )(lists, mob, vel, old, got2, coef, bur_wide, moved)


def solution(mesh):
    placed = (
        P(None, ("slab", "dom")),
        P(None, ("slab", "dom")),
        P(("slab", "dom")),
        P(("slab", "dom")),
        P(("slab", "dom"), None),
        P(("slab", "dom")),
    )
    return jax.shard_map(
        body,
        mesh=mesh,
        in_specs=placed,
        out_specs=(P(None, ("slab", "dom")), P(None, ("slab", "dom"))),
        check_vma=False,
    )
```

```python
import functools
import math

import jax
import jax.numpy as jnp
from jax import lax
from jax.experimental import pallas as pl
from jax.experimental.pallas import tpu as pltpu
from jax.sharding import PartitionSpec as P


LANES = 128
SUB = 8
CORE_NEAR = 0.25
CORE_FAR = 9.0
TIME_INCREMENT = 0.25
EXACT = lax.Precision.HIGHEST
VMEM = pl.BlockSpec(memory_space=pltpu.VMEM)
SMEM = pl.BlockSpec(memory_space=pltpu.SMEM)
HBM = pl.BlockSpec(memory_space=pltpu.HBM)
PARAMS = pltpu.CompilerParams(vmem_limit_bytes=8 * 1024 * 1024)
PARAMS_EVEN = pltpu.CompilerParams(vmem_limit_bytes=8 * 1024 * 1024)
SYM = ((0, 0), (0, 1), (0, 2), (1, 1), (1, 2), (2, 2))
MOMS = 3 + 9 + 18


def dot_lanes(a, b, precision=EXACT):
    return lax.dot_general(
        a, b, (((1,), (1,)), ((), ())), precision=precision, preferred_element_type=jnp.float32
    )


def center_of(cell):
    slab = jnp.floor(cell * 0.0625)
    rest = cell - 16.0 * slab
    row = jnp.floor(rest * 0.25)
    col = rest - 4.0 * row
    return (4.0 * slab + 2.0, 2.0 * row + 1.0, 2.0 * col + 1.0)


def put_cells(cells_smem, cell_ref):
    nblk = cells_smem.shape[0]
    lane = lax.broadcasted_iota(jnp.int32, (1, LANES), 1)
    last = jnp.zeros((1, LANES), jnp.float32)
    for b in range(nblk):
        cell = cells_smem[b].astype(jnp.float32)
        cell_ref[b : b + 1, :] = jnp.full((1, LANES), cell, jnp.float32)
        last = jnp.where(lane == MOMS * nblk + b, cell, last)
    cell_ref[nblk : nblk + 1, :] = last


def moment_row(pos, bur, cell_ref, stack_ref):
    nblk = pos[0].shape[0]
    z = center_of(cell_ref[0:nblk, :])
    d = [pos[k] - z[k] for k in range(3)]
    dd = [d[a] * d[e] for a, e in SYM]
    stack_ref[...] = jnp.zeros_like(stack_ref)
    m = 0
    for k in range(3):
        stack_ref[m * nblk : (m + 1) * nblk, :] = bur[k]
        m += 1
    for k in range(3):
        for a in range(3):
            stack_ref[m * nblk : (m + 1) * nblk, :] = bur[k] * d[a]
            m += 1
    for k in range(3):
        for j in range(6):
            stack_ref[m * nblk : (m + 1) * nblk, :] = bur[k] * dd[j]
            m += 1
    sums = dot_lanes(jnp.ones((SUB, LANES), jnp.float32), stack_ref[...])[0:1, :]
    lane = lax.broadcasted_iota(jnp.int32, (1, LANES), 1)
    return jnp.where(lane < MOMS * nblk, sums, cell_ref[nblk : nblk + 1, :])


def spread(out_ref, value):
    count = out_ref.shape[0]

    def put(d, carry):
        out_ref[d] = value
        return carry

    lax.fori_loop(0, count, put, 0, unroll=math.gcd(count, 32))


def first_kernel(
    count_ref, cells_hbm, pos_hbm, bur_hbm, pairs_hbm, mob_hbm,
    out_ref, win_ref, mob_ref, cell_ref,
    pos_ref, bur_ref, pairs_ref, cells_ref, stack_ref, load_ref, ids_ref, sem,
):
    moves = (
        (cells_hbm, cells_ref), (pos_hbm, pos_ref), (bur_hbm, bur_ref),
        (pairs_hbm, pairs_ref), (mob_hbm, mob_ref),
    )
    copies = [pltpu.make_async_copy(src, dst, sem.at[j]) for j, (src, dst) in enumerate(moves)]
    for copy in copies:
        copy.start()
    for copy in copies:
        copy.wait()
    nblk = cells_ref.shape[0]
    slots = pairs_ref.shape[1]
    pos, bur = [], []
    for k in range(3):
        for b in range(nblk):
            lanes = slice(b * LANES, (b + 1) * LANES)
            load_ref[k * nblk + b : k * nblk + b + 1, :] = pos_ref[k : k + 1, lanes]
            load_ref[(3 + k) * nblk + b : (3 + k) * nblk + b + 1, :] = bur_ref[k : k + 1, lanes]
    for k in range(3):
        pos.append(load_ref[k * nblk : (k + 1) * nblk, :])
        bur.append(load_ref[(3 + k) * nblk : (4 + k) * nblk, :])
    ids_ref[0:1, 0:slots] = pairs_ref[0:1, :]
    ids_ref[0:1, slots : 2 * slots] = pairs_ref[1:2, :]
    slot = lax.broadcasted_iota(jnp.int32, (1, LANES), 1)
    slot = jnp.where(slot < slots, slot, slot - slots)
    listed = jnp.where(slot < count_ref[0], ids_ref[0:1, :], -1).astype(jnp.float32)
    for r in range(6 * nblk):
        win_ref[0, :, r * LANES : (r + 1) * LANES] = load_ref[r : r + 1, :]
    win_ref[0, :, 6 * nblk * LANES :] = listed
    put_cells(cells_ref, cell_ref)
    spread(out_ref, moment_row(pos, bur, cell_ref, stack_ref))


def far_into(own_ref, bur_ref, mom_ref, center_ref, acc_ref, nblk, chunks):
    def visit(c, a, first):
        for t in range(LANES // SUB):
            rows = slice(t * SUB, (t + 1) * SUB)

            def mom(m):
                return mom_ref[c, m * nblk : m * nblk + 1, :]

            b = [bur_ref[a, k, rows, :] for k in range(3)]
            r = [own_ref[a, k, rows, :] - center_ref[c, k : k + 1, :] for k in range(3)]
            sq = r[0] * r[0] + r[1] * r[1] + (r[2] * r[2] + CORE_FAR)
            inv = lax.rsqrt(sq)
            inv2 = inv * inv
            inv3 = inv2 * inv
            q0 = b[0] * mom(0) + b[1] * mom(1) + b[2] * mom(2)
            q1 = [b[0] * mom(3 + e) + b[1] * mom(6 + e) + b[2] * mom(9 + e) for e in range(3)]
            q2 = [b[0] * mom(12 + j) + b[1] * mom(18 + j) + b[2] * mom(24 + j) for j in range(6)]
            u = [
                q2[0] * r[0] + q2[1] * r[1] + q2[2] * r[2],
                q2[1] * r[0] + q2[3] * r[1] + q2[4] * r[2],
                q2[2] * r[0] + q2[4] * r[1] + q2[5] * r[2],
            ]
            q1r = q1[0] * r[0] + q1[1] * r[1] + q1[2] * r[2]
            rqr = u[0] * r[0] + u[1] * r[1] + u[2] * r[2]
            trace = q2[0] + q2[3] + q2[5]
            inner = (3.0 * q1r - 0.5 * trace) + (2.5 * rqr) * inv2
            scal = q0 + inner * inv2
            for k in range(3):
                f = (r[k] * scal - (q1[k] + inv2 * u[k])) * inv3
                acc_ref[a, k, rows, :] = f if first else acc_ref[a, k, rows, :] + f

    def start(a, carry):
        visit(0, a, True)
        return carry

    def more(n, carry):
        visit(1 + n // nblk, n % nblk, False)
        return carry

    lax.fori_loop(0, nblk, start, 0)
    if chunks > 1:
        lax.fori_loop(0, nblk * (chunks - 1), more, 0)


def near_into(first_of, rows_at, coef_of, own_ref, used_of, acc_ref, nblk):
    for a in range(nblk):

        def ahead(n):
            return tuple(rows_at(first_of(a, 2 * n + j)) for j in range(2))

        def visit(n, carry):
            following = ahead(n + 1)
            p = [carry[j][:3] for j in range(2)]
            weigh = [coef_of(a, 2 * n + j, carry[j]) for j in range(2)]
            for t in range(LANES // SUB):
                rows = slice(t * SUB, (t + 1) * SUB)
                own = [own_ref[a, k, rows, :] for k in range(3)]
                f = []
                for j in range(2):
                    r = [own[k] - p[j][k] for k in range(3)]
                    sq = r[0] * r[0] + r[1] * r[1] + (r[2] * r[2] + CORE_NEAR)
                    u = lax.rsqrt(sq)
                    w = lax.rsqrt(sq + (CORE_FAR - CORE_NEAR))
                    wgt = weigh[j](t, rows) * (u * u * u - w * w * w)
                    f.append([wgt * r[k] for k in range(3)])
                for k in range(3):
                    acc_ref[a, k, rows, :] = acc_ref[a, k, rows, :] + (f[0][k] + f[1][k])
            return following

        lax.fori_loop(0, (used_of(a) + 1) // 2, visit, ahead(0))


def sum_lanes(acc_ref, force_ref, nblk):
    lane = lax.broadcasted_iota(jnp.int32, (SUB, LANES), 1)
    offset = lane - lax.broadcasted_iota(jnp.int32, (SUB, LANES), 0)
    for a in range(nblk):
        for k in range(3):
            out = jnp.zeros((SUB, LANES), jnp.float32)
            for t in range(LANES // SUB):
                total = jnp.sum(acc_ref[a, k, t * SUB : (t + 1) * SUB, :], axis=1, keepdims=True)
                out = jnp.where(offset == t * SUB, total, out)
            force_ref[k * nblk + a : k * nblk + a + 1, :] = jnp.sum(out, axis=0, keepdims=True)


def widen_own(row_of, own_ref, nblk):
    for a in range(nblk):
        for k in range(3):
            own_ref[a, k] = jnp.transpose(jnp.broadcast_to(row_of(k, a), (LANES, LANES)))


def window_ids(index, my_slab, my_dom, n_slab, n_dom, nblk):
    ids = jnp.full(index.shape, -2.0, jnp.float32)
    for k in range(9):
        s, e = my_slab + k // 3 - 1, my_dom + k % 3 - 1
        inside = (s >= 0) & (s < n_slab) & (e >= 0) & (e < n_dom)
        first = jnp.where(inside, (s * n_dom + e) * nblk - k * nblk, -100000)
        here = (index >= k * nblk) & (index < (k + 1) * nblk)
        ids = jnp.where(here, (index + first).astype(jnp.float32), ids)
    return ids


def build_lists(win_ref, rows, nblk, my_slab, my_dom, n_slab, n_dom, next_rows, count_ref, list_ref, mult_ref):
    high = -(-9 * nblk // SUB) * SUB
    place = (my_slab, my_dom, n_slab, n_dom, nblk)
    gid = window_ids(lax.broadcasted_iota(jnp.int32, (high, LANES), 0), *place)
    own = (my_slab * n_dom + my_dom) * nblk
    sub = lax.broadcasted_iota(jnp.int32, (SUB, LANES), 0)
    lane = lax.broadcasted_iota(jnp.int32, (SUB, LANES), 1)
    mine = jnp.where(sub < nblk, sub + own, -3).astype(jnp.float32)
    total = jnp.zeros((high, SUB), jnp.float32)
    for k in range(9):
        s, e = my_slab + k // 3 - 1, my_dom + k % 3 - 1
        inside = (s >= 0) & (s < n_slab) & (e >= 0) & (e < n_dom)
        row = jnp.where(inside, win_ref[k * rows + rows - 1], -1.0)
        other = pltpu.roll(row, LANES // 2, 1)
        left = (mine == row).astype(jnp.float32)
        right = (gid == other).astype(jnp.float32)
        total = total + dot_lanes(right, left, None)
    count_ref[...] = jnp.zeros_like(count_ref)
    count_ref[0:high, 0:SUB] = total
    count = jnp.transpose(count_ref[...])[0:SUB, :]
    met = jnp.where(count > 0.5, 1.0, 0.0)
    before = lax.broadcasted_iota(jnp.int32, (LANES, LANES), 0) < lax.broadcasted_iota(
        jnp.int32, (LANES, LANES), 1
    )
    rank = jnp.dot(met, before.astype(jnp.float32), preferred_element_type=jnp.float32)
    used = jnp.sum(met, axis=1, keepdims=True).astype(jnp.int32)
    list_ref[...] = jnp.where(lane == LANES - 1, used, 0)
    mult_ref[...] = jnp.zeros_like(mult_ref)
    line = window_ids(lane, *place)
    line = jnp.floor((line + 0.5) / nblk) * (next_rows - nblk) + line
    here = lane.astype(jnp.float32)
    here = jnp.floor((here + 0.5) / nblk) * (rows - nblk) + here
    spot = lax.broadcasted_iota(jnp.int32, (high, LANES), 0).astype(jnp.float32)
    line_high, here_high, count_high = (jnp.floor(x * 0.015625) for x in (line, here, count))
    line_low, here_low, count_low = line - 64.0 * line_high, here - 64.0 * here_high, count - 64.0 * count_high
    for a in range(nblk):
        pick = (rank[a : a + 1, :] == spot) & (met[a : a + 1, :] > 0.5)
        what = jnp.zeros((SUB, LANES), jnp.float32)
        parts = (line_high, line_low, here_high, here_low, count_high[a : a + 1, :], count_low[a : a + 1, :])
        for j, part in enumerate(parts):
            what = jnp.where(sub == j, part, what)
        out = dot_lanes(what, pick.astype(jnp.float32), None)
        list_ref[a : a + 1, 0:high] = (64.0 * out[0:1, :] + out[1:2, :] + 0.5).astype(jnp.int32)
        list_ref[nblk + a : nblk + a + 1, 0:high] = (64.0 * out[2:3, :] + out[3:4, :] + 0.5).astype(jnp.int32)
        mult_ref[a : a + 1, 0:high] = 64.0 * out[4:5, :] + out[5:6, :]


def gather_moments(got_ref, rows, mom_ref, center_ref, take_ref, nblk, ndev, far_scale):
    width = LANES // nblk
    for c in range(ndev // width):

        def take(d, carry):
            take_ref[pl.ds(d, 1), :] = got_ref[(c * width + d) * rows + rows - 1]
            return carry

        lax.fori_loop(0, width, take, 0, unroll=True)
        block = take_ref[...]
        turned = [block] + [pltpu.roll(block, LANES - b, 1) for b in range(1, nblk)]
        flat = jnp.transpose(jnp.concatenate(turned, axis=0))
        z = center_of(flat[MOMS * nblk : MOMS * nblk + 1, :])
        for k in range(3):
            center_ref[c, k : k + 1, :] = z[k]
        row = lax.broadcasted_iota(jnp.int32, (LANES, LANES), 0)
        mom_ref[c] = flat * jnp.where(row < 12 * nblk, far_scale, 3.0 * far_scale)


def second_kernel(
    n_slab, n_dom, far_scale,
    cell_ref, mob_ref, got_ref, low_ref, mid_ref, high_ref,
    own_ref, wide_ref,
    out_ref, vel_ref, list_ref, coef_ref, moved_ref, old_ref,
    stack_ref, acc_ref, force_ref, mom_ref, center_ref, take_ref,
    win_ref, count_ref, mult_ref, next_ref, flat_ref, list_smem, mult_smem, sem,
):
    nblk = mob_ref.shape[0]
    ndev = n_slab * n_dom
    rows = got_ref.shape[0] // ndev
    each = coef_ref.shape[0] // nblk
    my_slab, my_dom = lax.axis_index("slab"), lax.axis_index("dom")
    third = low_ref.shape[0]
    places = third // 3
    for j, ref in enumerate((low_ref, mid_ref, high_ref)):
        win_ref[j * third : (j + 1) * third] = ref[...]

    def own_row(k, b):
        return win_ref[4 * places + k * nblk + b]

    def own_bur(k, b):
        return own_row(3 + k, b)

    def first_of(a, e):
        return list_smem[nblk + a, e], mult_smem[a, e]

    def rows_at(found):
        first, mult = found
        rows = [win_ref[first + k * nblk] for k in range(6)]
        rows = rows[:3] + [row * mult for row in rows[3:]]
        return tuple(jnp.broadcast_to(row, (SUB, LANES)) for row in rows)

    def coef_of(a, e, found):
        def tile(t, rows):
            value = (
                wide_ref[a, 0, rows, :] * found[3]
                + wide_ref[a, 1, rows, :] * found[4]
                + wide_ref[a, 2, rows, :] * found[5]
            )
            coef_ref[a * each + e, rows, :] = value
            return value

        return tile

    build_lists(win_ref, places, nblk, my_slab, my_dom, n_slab, n_dom, 3 * nblk + 1, count_ref, list_ref, mult_ref)
    copies = [
        pltpu.make_async_copy(list_ref, list_smem, sem.at[0]),
        pltpu.make_async_copy(mult_ref, mult_smem, sem.at[1]),
    ]
    for copy in copies:
        copy.start()
    gather_moments(got_ref, rows, mom_ref, center_ref, take_ref, nblk, ndev, far_scale)
    far_into(own_ref, wide_ref, mom_ref, center_ref, acc_ref, nblk, mom_ref.shape[0])
    for copy in copies:
        copy.wait()
    near_into(first_of, rows_at, coef_of, own_ref, lambda a: list_smem[a, LANES - 1], acc_ref, nblk)
    sum_lanes(acc_ref, force_ref, nblk)
    pos, bur = [], []
    for k in range(3):
        here = slice(k * nblk, (k + 1) * nblk)
        vel = mob_ref[...] * force_ref[here, :]
        vel_ref[here, :] = vel
        for b in range(nblk):
            next_ref[k * nblk + b : k * nblk + b + 1, :] = own_row(k, b)
            next_ref[(3 + k) * nblk + b : (3 + k) * nblk + b + 1, :] = own_bur(k, b)
        old_ref[here, :] = next_ref[here, :]
        moved = next_ref[here, :] + TIME_INCREMENT * vel
        moved_ref[here, :] = moved
        pos.append(moved)
        bur.append(next_ref[(3 + k) * nblk : (4 + k) * nblk, :])
    last = moment_row(pos, bur, cell_ref, stack_ref)
    for r in range(3 * nblk):
        flat_ref[:, r * LANES : (r + 1) * LANES] = moved_ref[r : r + 1, :]
    flat_ref[:, 3 * nblk * LANES :] = last
    spread(out_ref, flat_ref[...])


def widen_kernel(row_ref, own_ref, wide_ref):
    nblk = own_ref.shape[0]
    widen_own(lambda k, b: row_ref[k * nblk + b], own_ref, nblk)
    widen_own(lambda k, b: row_ref[(3 + k) * nblk + b], wide_ref, nblk)


def third_kernel(
    n_slab, n_dom, far_scale,
    list_ref, mob_ref, vel_ref, old_ref, got_ref, coef_ref, wide_ref, next_ref,
    moved_ref, velocity_ref,
    own_ref, acc_ref, force_ref, mom_ref, center_ref, take_ref, list_smem, sem,
):
    copy = pltpu.make_async_copy(list_ref, list_smem, sem)
    copy.start()
    nblk = mob_ref.shape[0]
    ndev = n_slab * n_dom
    rows = got_ref.shape[0] // ndev
    each = coef_ref.shape[0] // nblk

    def first_of(a, e):
        return list_smem[a, e]

    def rows_at(first):
        return tuple(jnp.broadcast_to(got_ref[first + k * nblk], (SUB, LANES)) for k in range(3))

    def coef_of(a, e, found):
        return lambda t, rows: coef_ref[a * each + e, rows, :]

    widen_own(lambda k, b: next_ref[k * nblk + b : k * nblk + b + 1, :], own_ref, nblk)
    gather_moments(got_ref, rows, mom_ref, center_ref, take_ref, nblk, ndev, far_scale)
    far_into(own_ref, wide_ref, mom_ref, center_ref, acc_ref, nblk, mom_ref.shape[0])
    copy.wait()
    near_into(first_of, rows_at, coef_of, own_ref, lambda a: list_smem[a, LANES - 1], acc_ref, nblk)
    sum_lanes(acc_ref, force_ref, nblk)
    for k in range(3):
        here = slice(k * nblk, (k + 1) * nblk)
        force_ref[here, :] = 0.5 * (vel_ref[here, :] + mob_ref[...] * force_ref[here, :])
        for b in range(nblk):
            lanes = slice(b * LANES, (b + 1) * LANES)
            mean = force_ref[k * nblk + b : k * nblk + b + 1, :]
            velocity_ref[k : k + 1, lanes] = mean
            moved_ref[k : k + 1, lanes] = old_ref[k * nblk + b : k * nblk + b + 1, :] + TIME_INCREMENT * mean


def neighbours(x, axis):
    count = lax.axis_size(axis)
    above = lax.ppermute(x, axis, [((i + 1) % count, i) for i in range(count)])
    below = lax.ppermute(x, axis, [(i, (i + 1) % count) for i in range(count)])
    return below, above


def body(positions, burgers, mobility, block_cells, pairs, pair_count):
    f32 = jnp.float32
    segs = positions.shape[1]
    nblk = block_cells.shape[0]
    slots = pairs.shape[0]
    n_slab, n_dom = lax.axis_size("slab"), lax.axis_size("dom")
    ndev = n_slab * n_dom
    far_scale = math.sqrt(16 * n_slab / (segs * ndev))
    rows, places = 3 * nblk + 1, 6 * nblk + 1
    each = 9 * nblk + 2
    chunks = ndev * nblk // LANES
    high = -(-(3 * nblk) // SUB) * SUB
    wide = jax.ShapeDtypeStruct((nblk, 3, LANES, LANES), f32)
    payload = jax.ShapeDtypeStruct((ndev, 1, rows * LANES), f32)
    scratch = [
        pltpu.VMEM((nblk, 3, LANES, LANES), f32),
        pltpu.VMEM((high, LANES), f32),
        pltpu.VMEM((chunks, LANES, LANES), f32),
        pltpu.VMEM((chunks, SUB, LANES), f32),
        pltpu.VMEM((LANES // nblk, LANES), f32),
    ]
    load, window, mob, cells = pl.pallas_call(
        first_kernel,
        out_shape=(
            jax.ShapeDtypeStruct((ndev, 1, LANES), f32),
            jax.ShapeDtypeStruct((1, 1, places * LANES), f32),
            jax.ShapeDtypeStruct((nblk, LANES), f32),
            jax.ShapeDtypeStruct((SUB, LANES), f32),
        ),
        in_specs=[SMEM] + [HBM] * 5,
        out_specs=(VMEM,) * 4,
        scratch_shapes=[
            pltpu.VMEM((3, segs), f32),
            pltpu.VMEM((3, segs), f32),
            pltpu.VMEM((2, slots), jnp.int32),
            pltpu.SMEM((nblk,), jnp.int32),
            pltpu.VMEM((LANES, LANES), f32),
            pltpu.VMEM((-(-6 * nblk // SUB) * SUB, LANES), f32),
            pltpu.VMEM((SUB, LANES), jnp.int32),
            pltpu.SemaphoreType.DMA((5,)),
        ],
        compiler_params=PARAMS,
        name="pack",
    )(
        pair_count,
        *(
            pltpu.with_memory_space_constraint(x, pltpu.HBM)
            for x in (block_cells, positions, burgers, pairs.T, mobility.reshape(nblk, LANES))
        ),
    )
    got = lax.all_to_all(load, ("slab", "dom"), 0, 0, tiled=True)
    below, above = neighbours(window, "dom")
    row = jnp.concatenate([below, window, above], axis=0)
    left, right = neighbours(row, "slab")
    left, row, right = (x.reshape(3 * places, 1, LANES) for x in (left, row, right))
    pos_wide, bur_wide = pl.pallas_call(
        widen_kernel,
        out_shape=(wide, wide),
        in_specs=[VMEM],
        out_specs=(VMEM, VMEM),
        compiler_params=PARAMS,
        name="widen",
    )(window.reshape(places, 1, LANES))
    load2, vel, lists, coef, moved, old = pl.pallas_call(
        functools.partial(second_kernel, n_slab, n_dom, far_scale),
        out_shape=(
            payload,
            jax.ShapeDtypeStruct((3 * nblk, LANES), f32),
            jax.ShapeDtypeStruct((SUB, LANES), jnp.int32),
            jax.ShapeDtypeStruct((nblk * each, LANES, LANES), f32),
            jax.ShapeDtypeStruct((3 * nblk, LANES), f32),
            jax.ShapeDtypeStruct((3 * nblk, LANES), f32),
        ),
        in_specs=[VMEM] * 8,
        out_specs=(VMEM,) * 6,
        scratch_shapes=[pltpu.VMEM((LANES, LANES), f32)]
        + scratch
        + [
            pltpu.VMEM((9 * places, 1, LANES), f32),
            pltpu.VMEM((LANES, LANES), f32),
            pltpu.VMEM((SUB, LANES), f32),
            pltpu.VMEM((6 * nblk, LANES), f32),
            pltpu.VMEM((1, rows * LANES), f32),
            pltpu.SMEM((SUB, LANES), jnp.int32),
            pltpu.SMEM((SUB, LANES), f32),
            pltpu.SemaphoreType.DMA((2,)),
        ],
        compiler_params=PARAMS,
        name="step_one",
    )(cells, mob, got, left, row, right, pos_wide, bur_wide)
    got2 = lax.all_to_all(load2, ("slab", "dom"), 0, 0, tiled=True).reshape(ndev * rows, 1, LANES)
    return pl.pallas_call(
        functools.partial(third_kernel, n_slab, n_dom, far_scale),
        out_shape=(jax.ShapeDtypeStruct((3, segs), f32),) * 2,
        in_specs=[VMEM] * 8,
        out_specs=(VMEM, VMEM),
        scratch_shapes=[pltpu.VMEM((nblk, 3, LANES, LANES), f32)]
        + scratch
        + [pltpu.SMEM((SUB, LANES), jnp.int32), pltpu.SemaphoreType.DMA(())],
        compiler_params=PARAMS_EVEN,
        name="step_two",
    )(lists, mob, vel, old, got2, coef, bur_wide, moved)


def solution(mesh):
    placed = (
        P(None, ("slab", "dom")),
        P(None, ("slab", "dom")),
        P(("slab", "dom")),
        P(("slab", "dom")),
        P(("slab", "dom"), None),
        P(("slab", "dom")),
    )
    return jax.shard_map(
        body,
        mesh=mesh,
        in_specs=placed,
        out_specs=(P(None, ("slab", "dom")), P(None, ("slab", "dom"))),
        check_vma=False,
    )
```
